32 devices in a mesh: groups: 2 (over x), tok: 8 (over z, y), dom: 2 (over core).
Axes of the slice: x: 2, y: 2, z: 4, core: 2. Of those that a mesh axis runs over, the one named last changes fastest.
Arguments:
- states: bfloat16 [32, 128, 768], P(('groups', 'dom'), 'tok'), parts along dimension 0, may hold values from -12 to 12
- ancestors: int32 [32], P(('groups', 'dom')), parts along dimension 0, may hold values from 0 to 15, as said below
- noise: bfloat16 [32, 128, 768], P(('groups', 'dom'), 'tok'), parts along dimension 0, may hold values from -6 to 6
- pair: bfloat16 [256, 128, 128], P(('groups', 'tok')), parts along dimension 0, may hold values from -200 to 200
- token_mask: int32 [256], P('groups'), parts along dimension 0, may hold values 0 or 1
- w_qkv: bfloat16 [2, 768, 2304], replicated, may hold values from -0.21875 to 0.21875
- w_out: bfloat16 [2, 768, 768], replicated, may hold values from -0.21875 to 0.21875
- w_pair: bfloat16 [2, 128, 16], replicated, may hold values from -1.5 to 1.5
Outputs:
- new_states: bfloat16 [32, 128, 768], P(('groups', 'dom'), 'tok'), parts along dimension 0
The draws below stay inside these ranges and needn't reach their ends.
There are 2 independent parts, one for each index of `groups`. The reference program is written for one: setup_inputs(seed, part) draws one part's arguments, and reference() takes and returns one part's arrays. A program takes and returns all parts, laid end to end along the dimension named above; an argument that names none is the same for every part. Nothing has to cross between parts.
Inputs may be any that keep to these rules, and one draw needn't show every extreme that they name: `ancestors`: nondecreasing over particles; the first entry is 0 and the last is 15.
All inputs are finite; a program needn't handle non-finite values.
Results may differ from the reference program's by a relative error of at most 0.015.
Values may be sent and summed in bfloat16 or wider, within the bound.
No kernel may reach another device: no remote copies, remote signals or barrier semaphores. Data moves between devices by JAX's collectives and lax.ppermute only.
A program may use at most 128 MiB of HBM per device.

```python
import jax
import jax.numpy as jnp
from jax import lax

D = 768
HEADS = 16
C_PAIR = 128
LAYERS = 2
HEAD_DIM = 48
TOKENS = 128
PARTICLES = 16


def draw_states(key, part):
    key_base = jax.random.fold_in(key, 0)
    shape = (PARTICLES, TOKENS, D)
    result = jnp.clip(jax.random.normal(key_base, shape, jnp.float32), -6.0, 6.0)
    return result.astype(jnp.bfloat16)


def draw_pair(key, part):
    key_base = jax.random.fold_in(key, 0)
    shape = (TOKENS, TOKENS, C_PAIR)
    result = jnp.clip(jax.random.normal(key_base, shape, jnp.float32), -6.0, 6.0)
    return result.astype(jnp.bfloat16)


def draw_ancestors(key, part):
    picked = jnp.sort(jax.random.randint(key, (PARTICLES,), 0, PARTICLES))
    picked = picked.at[0].set(0)
    picked = picked.at[PARTICLES - 1].set(PARTICLES - 1)
    return picked.astype(jnp.int32)


def place_ends(entries, own_key, low, top_value):
    longest = entries.shape.index(max(entries.shape))
    spots = []
    for shift in (0, 1):
        where = [jax.random.randint(jax.random.fold_in(own_key, axis), (), 0, length) for axis, length in enumerate(entries.shape)]
        where[longest] = (where[longest] + shift) % entries.shape[longest]
        spots.append(tuple(where))
    return entries.at[spots[0]].set(low).at[spots[1]].set(top_value)


def block_scale(stream_key, shape, cuts, low, largest):
    factor_of, own = 1.0, jax.random.fold_in(stream_key, 6)
    for axis_at, shards_of in cuts:
        heights = jnp.exp(jax.random.uniform(jax.random.fold_in(own, axis_at), (shards_of,), jnp.float32, low / len(cuts), largest / len(cuts)))
        factor_of = factor_of * jnp.repeat(heights, shape[axis_at] // shards_of).reshape([-1 if axis == axis_at else 1 for axis in range(len(shape))])
    return factor_of


def normal_values(rng, shape, deviation, limit, cuts=(), kind=jnp.bfloat16):
    values = jax.random.normal(rng, shape, jnp.float32) * deviation
    if len(cuts) > 0:
        values = block_scale(rng, shape, cuts, -0.22, 0.18) * values
    return jnp.clip(values, min=-limit, max=limit).astype(kind)


def setup_inputs(seed: int = 0, part: int = 0) -> dict:
    keys = jax.random.split(jax.random.key(seed), 9)
    own_keys = jax.random.split(jax.random.fold_in(keys[8], part), 9)
    states = draw_states(jax.random.fold_in(jax.random.fold_in(keys[8], part), 71), part)
    ancestors = draw_ancestors(jax.random.fold_in(jax.random.fold_in(keys[8], part), 71), part)
    noise = normal_values(own_keys[2], (PARTICLES, TOKENS, D), 1.0, 6.0, ((0, 2), (1, 8)))
    pair = draw_pair(jax.random.fold_in(jax.random.fold_in(keys[8], part), 71), part)
    token_mask = place_ends((jax.random.randint(own_keys[4], (TOKENS,), 0, 8) < 7).astype(jnp.int32), jax.random.fold_in(own_keys[4], 1), 0, 1)
    w_qkv = normal_values(keys[5], (LAYERS, D, 3 * D), D ** -0.5, 0.21875)
    w_out = normal_values(keys[6], (LAYERS, D, D), D ** -0.5, 0.21875)
    w_pair = normal_values(keys[7], (LAYERS, C_PAIR, HEADS), 0.25, 1.5)
    return {"states": states, "ancestors": ancestors, "noise": noise, "pair": pair, "token_mask": token_mask, "w_qkv": w_qkv, "w_out": w_out, "w_pair": w_pair}


def layer_norm(stream):
    values = stream.astype(jnp.float32)
    average = lax.optimization_barrier(jnp.mean(values, axis=-1, keepdims=True))
    centred = values - average
    spread = lax.optimization_barrier(jnp.mean(centred * centred, axis=-1, keepdims=True))
    return centred * lax.rsqrt(spread + 1e-05)

def attend_one(query_one, key_one, value_one, full_bias):
    scores = jnp.einsum('ihe,jhe->hij', query_one.astype(jnp.float32), key_one.astype(jnp.float32)) + full_bias
    weights = jax.nn.softmax(scores, axis=-1).astype(jnp.bfloat16)
    return jnp.einsum('hij,jhe->ihe', weights.astype(jnp.float32), value_one.astype(jnp.float32)).astype(jnp.bfloat16)

def reference(states, ancestors, noise, pair, token_mask, w_qkv, w_out, w_pair):
    chosen = jnp.take(states, ancestors, axis=0)
    stream = (chosen.astype(jnp.float32) + 0.5 * noise.astype(jnp.float32)).astype(jnp.bfloat16)
    penalty = jnp.where(token_mask > 0, 0.0, -1000000000.0).astype(jnp.float32)
    pair_wide = pair.astype(jnp.float32)
    query_scale = HEAD_DIM ** (-0.5)
    for layer_index in range(LAYERS):
        full_bias = jnp.einsum('ijc,ch->hij', pair_wide, w_pair[layer_index].astype(jnp.float32)) + penalty[None, None, :]
        normed = layer_norm(stream).astype(jnp.bfloat16)
        projected = jnp.dot(normed.reshape(PARTICLES * TOKENS, D), w_qkv[layer_index], preferred_element_type=jnp.float32)
        projected = projected.reshape(PARTICLES, TOKENS, 3 * D)
        query = (projected[..., :D] * query_scale).astype(jnp.bfloat16).reshape(PARTICLES, TOKENS, HEADS, HEAD_DIM)
        key_rows = projected[..., D:2 * D].astype(jnp.bfloat16).reshape(PARTICLES, TOKENS, HEADS, HEAD_DIM)
        value_rows = projected[..., 2 * D:].astype(jnp.bfloat16).reshape(PARTICLES, TOKENS, HEADS, HEAD_DIM)
        attended = lax.map(lambda trio: attend_one(trio[0], trio[1], trio[2], full_bias), (query, key_rows, value_rows))
        attended = attended.reshape(PARTICLES * TOKENS, D)
        update = jnp.dot(attended, w_out[layer_index], preferred_element_type=jnp.float32).reshape(PARTICLES, TOKENS, D)
        stream = (stream.astype(jnp.float32) + update).astype(jnp.bfloat16)
    return stream
```

```python
import jax
import jax.numpy as jnp
from jax import lax
from jax.experimental import pallas as pl
from jax.experimental.pallas import tpu as pltpu
from jax.sharding import PartitionSpec as P

MASKED = -1000000000.0
LANES = 128


def layer_norm(stream):
    values = stream.astype(jnp.float32)
    average = jnp.mean(values, axis=-1, keepdims=True)
    centred = values - average
    spread = jnp.mean(centred * centred, axis=-1, keepdims=True)
    return centred * lax.rsqrt(spread + 1e-05)


def gathered_body(states, ancestors, noise, pair, token_mask, w_qkv, w_out, w_pair):
    part_count = states.shape[0]
    tok_rows = states.shape[1]
    model_width = states.shape[2]
    head_count = w_pair.shape[2]
    head_width = model_width // head_count
    layer_count = w_qkv.shape[0]
    total_keys = pair.shape[1]
    everyone = lax.all_gather(states, "dom", axis=0, tiled=True)
    chosen = jnp.take(everyone, ancestors, axis=0)
    stream = (chosen.astype(jnp.float32) + 0.5 * noise.astype(jnp.float32)).astype(jnp.bfloat16)
    penalty = jnp.where(token_mask > 0, 0.0, MASKED).astype(jnp.float32)
    pair_terms = jnp.einsum("ijc,lch->lhij", pair, w_pair, preferred_element_type=jnp.float32)
    full_bias = pair_terms + penalty[None, None, None, :]
    query_scale = head_width ** (-0.5)
    for layer_index in range(layer_count):
        normed = layer_norm(stream).astype(jnp.bfloat16)
        projected = jnp.dot(
            normed.reshape(part_count * tok_rows, model_width),
            w_qkv[layer_index],
            preferred_element_type=jnp.float32,
        )
        projected = projected.reshape(part_count, tok_rows, 3 * model_width)
        query = (projected[..., :model_width] * query_scale).astype(jnp.bfloat16)
        both = projected[..., model_width:].astype(jnp.bfloat16)
        query_heads = query.reshape(part_count, tok_rows, head_count, head_width)
        gathered = lax.all_gather(both, "tok", axis=1, tiled=True)
        all_keys, all_values = gathered[..., :model_width], gathered[..., model_width:]
        key_heads = all_keys.reshape(part_count, total_keys, head_count, head_width)
        scores = (
            jnp.einsum(
                "pihe,pjhe->phij", query_heads, key_heads, preferred_element_type=jnp.float32
            )
            + full_bias[layer_index][None]
        )
        weights = jax.nn.softmax(scores, axis=-1).astype(jnp.bfloat16)
        value_heads = all_values.reshape(part_count, total_keys, head_count, head_width)
        attended = jnp.einsum(
            "phij,pjhe->pihe", weights, value_heads, preferred_element_type=jnp.float32
        ).astype(jnp.bfloat16)
        attended = attended.reshape(part_count * tok_rows, model_width)
        update = jnp.dot(attended, w_out[layer_index], preferred_element_type=jnp.float32)
        update = update.reshape(part_count, tok_rows, model_width)
        stream = (stream.astype(jnp.float32) + update).astype(jnp.bfloat16)
    return stream


def whole_vmem():
    return pl.BlockSpec(memory_space=pltpu.VMEM)


def in_hbm():
    return pl.BlockSpec(memory_space=pl.ANY)


def in_smem():
    return pl.BlockSpec(memory_space=pltpu.SMEM)


def make_bias(pair, mask_row, w_rows, particles, stream_rows):
    rows, keys, _ = pair.shape
    heads = w_rows.shape[0]

    def kernel(pair_ref, mask_ref, w_ref, out_ref, rows_ref):
        penalty = jnp.where(mask_ref[...] > 0, 0.0, MASKED).astype(jnp.float32)
        for i in range(rows):
            piece = lax.dot_general(
                w_ref[...], pair_ref[i], (((1,), (1,)), ((), ())),
                preferred_element_type=jnp.float32,
            ) + penalty
            rows_ref[:, i, :] = piece - jnp.max(piece, axis=-1, keepdims=True)
        for h in range(heads):
            block = rows_ref[h].astype(jnp.bfloat16)
            for p in range(particles):
                out_ref[p, stream_rows + h * rows : stream_rows + (h + 1) * rows, :] = block

    return pl.pallas_call(
        kernel,
        out_shape=jax.ShapeDtypeStruct((particles, stream_rows + heads * rows, keys), jnp.bfloat16),
        in_specs=[whole_vmem(), whole_vmem(), whole_vmem()],
        out_specs=whole_vmem(),
        scratch_shapes=[pltpu.VMEM((heads, rows, keys), jnp.float32)],
        cost_estimate=pl.CostEstimate(
            flops=2 * heads * rows * keys * LANES, transcendentals=0, bytes_accessed=2000000
        ),
        name="make_bias",
    )(pair, mask_row, w_rows)


def add_stream(dom, ancestors, own, other, noise, packed):
    particles, rows, width = own.shape

    def kernel(dom_ref, anc_ref, own_ref, other_ref, noise_ref, packed_ref, out_ref):
        del packed_ref
        for p in range(particles):
            a = anc_ref[p]
            local = lax.rem(a, particles)
            mine = lax.div(a, particles) == dom_ref[0]
            value = jnp.where(mine, own_ref[local], other_ref[local])
            value = value.astype(jnp.float32) + 0.5 * noise_ref[p].astype(jnp.float32)
            value = value.astype(jnp.bfloat16)
            for k in range(width // LANES):
                out_ref[p, k * rows : (k + 1) * rows, :] = value[:, k * LANES : (k + 1) * LANES]

    used = rows * (width // LANES)
    free_rows = pl.BlockSpec((particles, used, LANES), lambda i: (0, 0, 0))
    return pl.pallas_call(
        kernel,
        out_shape=jax.ShapeDtypeStruct(packed.shape, packed.dtype),
        in_specs=[in_smem(), in_smem(), whole_vmem(), whole_vmem(), whole_vmem(), in_hbm()],
        out_specs=free_rows,
        grid=(1,),
        input_output_aliases={5: 0},
        name="add_stream",
    )(dom, ancestors, own, other, noise, packed)


def project(normed, w_buf, q_ref, k_ref, v_ref, width, scale):
    q_ref[...] = (
        jnp.dot(normed, w_buf[:, :width], preferred_element_type=jnp.float32) * scale
    ).astype(jnp.bfloat16)
    k_ref[...] = jnp.dot(
        normed, w_buf[:, width : 2 * width], preferred_element_type=jnp.float32
    ).astype(jnp.bfloat16)
    v_ref[...] = jnp.dot(
        normed, w_buf[:, 2 * width :], preferred_element_type=jnp.float32
    ).astype(jnp.bfloat16)


def first_project(received, w_qkv, rows, width, scale):
    sources = received.shape[0]
    tokens = sources * rows

    def kernel(recv_ref, w_hbm, x_ref, q_ref, k_ref, v_ref, w_buf, sem):
        copies = []
        for n in range(3):
            cols = pl.ds(n * width, width)
            copies.append(
                pltpu.make_async_copy(w_hbm.at[0, :, cols], w_buf.at[:, cols], sem.at[n])
            )
            copies[n].start()
        for s in range(sources):
            for k in range(width // LANES):
                x_ref[s * rows : (s + 1) * rows, k * LANES : (k + 1) * LANES] = recv_ref[
                    s, k * rows : (k + 1) * rows, :
                ]
        normed = layer_norm(x_ref[...]).astype(jnp.bfloat16)
        for n, ref in enumerate((q_ref, k_ref, v_ref)):
            copies[n].wait()
            value = jnp.dot(
                normed, w_buf[:, n * width : (n + 1) * width], preferred_element_type=jnp.float32
            )
            if n == 0:
                value = value * scale
            ref[...] = value.astype(jnp.bfloat16)

    shape = jax.ShapeDtypeStruct((tokens, width), jnp.bfloat16)
    return pl.pallas_call(
        kernel,
        out_shape=(shape,) * 4,
        in_specs=[whole_vmem(), in_hbm()],
        out_specs=(whole_vmem(),) * 4,
        scratch_shapes=[
            pltpu.VMEM((width, 3 * width), jnp.bfloat16),
            pltpu.SemaphoreType.DMA((3,)),
        ],
        compiler_params=pltpu.CompilerParams(vmem_limit_bytes=24 * 2**20),
        cost_estimate=pl.CostEstimate(
            flops=6 * tokens * width * width, transcendentals=0, bytes_accessed=8 * width * width
        ),
        name="first_project",
    )(received, w_qkv)


def layers(dom, mask, stream, query, keys, values, received, other, w_qkv, w_out, rows, heads, scale):
    tokens, width = stream.shape
    layer_count = w_qkv.shape[0]
    sources = received.shape[0]
    head_width = width // heads
    half = heads // 2
    stream_rows = rows * (width // LANES)

    def kernel(
        dom_ref, mask_ref, x_ref, q_in, k_in, v_in, recv_ref, other_ref, wq_hbm, wo_hbm,
        out_ref, x_buf, q_buf, k_buf, v_buf, att_buf, wq_buf, wo_buf, wq_sem, wo_sem,
    ):
        wo_copies = [
            pltpu.make_async_copy(wo_hbm.at[l], wo_buf.at[l], wo_sem.at[l])
            for l in range(layer_count)
        ]
        wq_copies = [
            pltpu.make_async_copy(wq_hbm.at[l], wq_buf.at[l - 1], wq_sem.at[l - 1])
            for l in range(1, layer_count)
        ]
        wo_copies[0].start()
        for l in range(1, layer_count):
            wq_copies[l - 1].start()
            wo_copies[l].start()
        is_first = dom_ref[0] == 0
        anyone = jnp.max(mask_ref[...], axis=-1, keepdims=True)
        floor = jnp.where(anyone > 0, 0.0, MASKED).astype(jnp.float32)

        for l in range(layer_count):
            q_ref, k_ref, v_ref = (q_in, k_in, v_in) if l == 0 else (q_buf, k_buf, v_buf)
            stream_ref = x_ref if l == 0 else x_buf
            for h in range(heads):
                low = h * head_width
                high = low + head_width
                start = low // LANES * LANES
                stop = -(-high // LANES) * LANES
                lane = lax.broadcasted_iota(jnp.int32, (tokens, stop - start), 1) + start
                inside = (lane >= low) & (lane < high)
                q_head = jnp.where(inside, q_ref[:, start:stop].astype(jnp.float32), 0.0)
                scores = lax.dot_general(
                    q_head.astype(jnp.bfloat16), k_ref[:, start:stop], (((1,), (1,)), ((), ())),
                    preferred_element_type=jnp.float32,
                )
                base = stream_rows + (l * half + h % half) * rows
                near = recv_ref[:, base : base + rows, :].reshape(tokens, tokens)
                far = other_ref[:, base : base + rows, :].reshape(tokens, tokens)
                bias = jnp.where(is_first, near, far) if h < half else jnp.where(is_first, far, near)
                scores = scores + (bias.astype(jnp.float32) + floor)
                top = jnp.max(scores, axis=-1, keepdims=True)
                raised = jnp.exp(scores - top)
                total = jnp.sum(raised, axis=-1, keepdims=True)
                weights = (raised / total).astype(jnp.bfloat16)
                out = jnp.dot(weights, v_ref[:, start:stop], preferred_element_type=jnp.float32)
                if low == start:
                    att_buf[:, start:stop] = out
                else:
                    for t in range(start, stop, LANES):
                        piece = out[:, t - start : t - start + LANES]
                        if t >= low:
                            att_buf[:, t : t + LANES] = piece
                        else:
                            att_buf[:, t : t + LANES] = jnp.where(
                                inside[:, t - start : t - start + LANES], piece,
                                att_buf[:, t : t + LANES],
                            )
            wo_copies[l].wait()
            update = jnp.dot(
                att_buf[...].astype(jnp.bfloat16), wo_buf[l], preferred_element_type=jnp.float32
            )
            moved = (stream_ref[...].astype(jnp.float32) + update).astype(jnp.bfloat16)
            if l + 1 < layer_count:
                x_buf[...] = moved
                normed = layer_norm(moved).astype(jnp.bfloat16)
                wq_copies[l].wait()
                project(normed, wq_buf.at[l], q_buf, k_buf, v_buf, width, scale)
            else:
                for s in range(sources):
                    out_ref[s] = moved[s * rows : (s + 1) * rows, :]

    wide = pltpu.VMEM((tokens, width), jnp.bfloat16)
    return pl.pallas_call(
        kernel,
        out_shape=jax.ShapeDtypeStruct((sources, rows, width), jnp.bfloat16),
        in_specs=[in_smem()] + [whole_vmem()] * 7 + [in_hbm()] * 2,
        out_specs=whole_vmem(),
        scratch_shapes=[
            wide, wide, wide, wide, pltpu.VMEM((tokens, width), jnp.float32),
            pltpu.VMEM((layer_count - 1, width, 3 * width), jnp.bfloat16),
            pltpu.VMEM((layer_count, width, width), jnp.bfloat16),
            pltpu.SemaphoreType.DMA((layer_count - 1,)),
            pltpu.SemaphoreType.DMA((layer_count,)),
        ],
        compiler_params=pltpu.CompilerParams(vmem_limit_bytes=32 * 2**20),
        cost_estimate=pl.CostEstimate(
            flops=14 * tokens * width * width, transcendentals=2 * heads * tokens * tokens,
            bytes_accessed=10 * width * width,
        ),
        name="layers",
    )(dom, mask, stream, query, keys, values, received, other, w_qkv, w_out)


def spread_body(states, ancestors, noise, pair, token_mask, w_qkv, w_out, w_pair):
    particles, rows, width = states.shape
    layer_count, channels, heads = w_pair.shape
    half = heads // 2
    scale = (width // heads) ** (-0.5)
    stream_rows = rows * (width // LANES)
    swap = [(0, 1), (1, 0)]
    here = lax.axis_index("dom")
    dom = here.astype(jnp.int32).reshape(1)
    mask_row = token_mask.reshape(1, -1)
    other_states = lax.ppermute(states, "dom", swap)
    w_rows = lax.dynamic_slice_in_dim(w_pair.transpose(0, 2, 1), here * half, half, axis=1)
    packed = make_bias(
        pair, mask_row, w_rows.reshape(layer_count * half, channels), particles, stream_rows
    )
    packed = add_stream(dom, ancestors, states, other_states, noise, packed)
    received = lax.all_to_all(packed, "tok", 0, 0, tiled=True)
    other = lax.ppermute(received, "dom", swap)
    stream, query, keys, values = first_project(received, w_qkv, rows, width, scale)
    result = layers(
        dom, mask_row, stream, query, keys, values, received, other, w_qkv, w_out, rows, heads, scale
    )
    return lax.all_to_all(result, "tok", 0, 0, tiled=True)


def solution(mesh):
    placed = (
        P(("groups", "dom"), "tok", None),
        P(("groups", "dom")),
        P(("groups", "dom"), "tok", None),
        P(("groups", "tok"), None, None),
        P("groups"),
        P(),
        P(),
        P(),
    )

    def body(states, ancestors, noise, pair, token_mask, w_qkv, w_out, w_pair):
        particles, rows, width = states.shape
        fits = (
            particles == mesh.shape["tok"]
            and mesh.shape["dom"] == 2
            and w_pair.shape[2] % 2 == 0
            and pair.shape[1] == LANES
            and pair.shape[2] == LANES
            and width % LANES == 0
            and rows % 16 == 0
        )
        chosen = spread_body if fits else gathered_body
        return chosen(states, ancestors, noise, pair, token_mask, w_qkv, w_out, w_pair)

    return jax.shard_map(
        body,
        mesh=mesh,
        in_specs=placed,
        out_specs=P(("groups", "dom"), "tok", None),
        check_vma=False,
    )
```

```python
import jax
import jax.numpy as jnp
from jax import lax
from jax.experimental import pallas as pl
from jax.experimental.pallas import tpu as pltpu
from jax.sharding import PartitionSpec as P

MASKED = -1000000000.0
LANES = 128


def layer_norm(stream):
    values = stream.astype(jnp.float32)
    average = jnp.mean(values, axis=-1, keepdims=True)
    centred = values - average
    spread = jnp.mean(centred * centred, axis=-1, keepdims=True)
    return centred * lax.rsqrt(spread + 1e-05)


def gathered_body(states, ancestors, noise, pair, token_mask, w_qkv, w_out, w_pair):
    part_count = states.shape[0]
    tok_rows = states.shape[1]
    model_width = states.shape[2]
    head_count = w_pair.shape[2]
    head_width = model_width // head_count
    layer_count = w_qkv.shape[0]
    total_keys = pair.shape[1]
    everyone = lax.all_gather(states, "dom", axis=0, tiled=True)
    chosen = jnp.take(everyone, ancestors, axis=0)
    stream = (chosen.astype(jnp.float32) + 0.5 * noise.astype(jnp.float32)).astype(jnp.bfloat16)
    penalty = jnp.where(token_mask > 0, 0.0, MASKED).astype(jnp.float32)
    pair_terms = jnp.einsum("ijc,lch->lhij", pair, w_pair, preferred_element_type=jnp.float32)
    full_bias = pair_terms + penalty[None, None, None, :]
    query_scale = head_width ** (-0.5)
    for layer_index in range(layer_count):
        normed = layer_norm(stream).astype(jnp.bfloat16)
        projected = jnp.dot(
            normed.reshape(part_count * tok_rows, model_width),
            w_qkv[layer_index],
            preferred_element_type=jnp.float32,
        )
        projected = projected.reshape(part_count, tok_rows, 3 * model_width)
        query = (projected[..., :model_width] * query_scale).astype(jnp.bfloat16)
        both = projected[..., model_width:].astype(jnp.bfloat16)
        query_heads = query.reshape(part_count, tok_rows, head_count, head_width)
        gathered = lax.all_gather(both, "tok", axis=1, tiled=True)
        all_keys, all_values = gathered[..., :model_width], gathered[..., model_width:]
        key_heads = all_keys.reshape(part_count, total_keys, head_count, head_width)
        scores = (
            jnp.einsum(
                "pihe,pjhe->phij", query_heads, key_heads, preferred_element_type=jnp.float32
            )
            + full_bias[layer_index][None]
        )
        weights = jax.nn.softmax(scores, axis=-1).astype(jnp.bfloat16)
        value_heads = all_values.reshape(part_count, total_keys, head_count, head_width)
        attended = jnp.einsum(
            "phij,pjhe->pihe", weights, value_heads, preferred_element_type=jnp.float32
        ).astype(jnp.bfloat16)
        attended = attended.reshape(part_count * tok_rows, model_width)
        update = jnp.dot(attended, w_out[layer_index], preferred_element_type=jnp.float32)
        update = update.reshape(part_count, tok_rows, model_width)
        stream = (stream.astype(jnp.float32) + update).astype(jnp.bfloat16)
    return stream


def whole_vmem():
    return pl.BlockSpec(memory_space=pltpu.VMEM)


def in_hbm():
    return pl.BlockSpec(memory_space=pltpu.HBM)


def stay(array):
    return pltpu.with_memory_space_constraint(array, pltpu.HBM)


def in_smem():
    return pl.BlockSpec(memory_space=pltpu.SMEM)


def prepare(pair, mask_row, w_rows, own, noise, w_qkv):
    rows, keys, channels = pair.shape
    layer_count, heads, _ = w_rows.shape
    half = heads // 2
    blocks = layer_count * half

    def kernel(
        pair_hbm, mask_hbm, w_hbm, own_hbm, noise_hbm, wq_hbm,
        bias_ref, own_ref, noise_ref, first_ref, pair_ref, mask_ref, w_ref, rows_ref, sem,
    ):
        copies = [
            pltpu.make_async_copy(mask_hbm, mask_ref, sem.at[0]),
            pltpu.make_async_copy(w_hbm, w_ref, sem.at[1]),
            pltpu.make_async_copy(pair_hbm, pair_ref, sem.at[2]),
            pltpu.make_async_copy(own_hbm, own_ref, sem.at[3]),
            pltpu.make_async_copy(noise_hbm, noise_ref, sem.at[4]),
            pltpu.make_async_copy(wq_hbm.at[0], first_ref, sem.at[5]),
        ]
        for copy in copies:
            copy.start()
        copies[0].wait()
        copies[1].wait()
        penalty = jnp.where(mask_ref[...] > 0, 0.0, MASKED).astype(jnp.float32)
        is_first = lax.axis_index("dom") == 0
        sent = jnp.concatenate(
            [
                jnp.where(is_first, w[:half], w[half:])
                for w in (w_ref[l].astype(jnp.float32) for l in range(layer_count))
            ],
            axis=0,
        ).astype(jnp.bfloat16)
        copies[2].wait()
        for i in range(rows):
            piece = across(sent, pair_ref[i]) + penalty
            rows_ref[:, i, :] = piece - jnp.max(piece, axis=-1, keepdims=True)
        for h in range(blocks):
            bias_ref[h * rows : (h + 1) * rows, :] = rows_ref[h].astype(jnp.bfloat16)
        for copy in copies[3:]:
            copy.wait()

    return pl.pallas_call(
        kernel,
        out_shape=(
            jax.ShapeDtypeStruct((blocks * rows, keys), jnp.bfloat16),
            jax.ShapeDtypeStruct(own.shape, own.dtype),
            jax.ShapeDtypeStruct(noise.shape, noise.dtype),
            jax.ShapeDtypeStruct(w_qkv.shape[1:], w_qkv.dtype),
        ),
        in_specs=[in_hbm()] * 6,
        out_specs=(whole_vmem(),) * 4,
        scratch_shapes=[
            pltpu.VMEM(pair.shape, pair.dtype),
            pltpu.VMEM(mask_row.shape, mask_row.dtype),
            pltpu.VMEM(w_rows.shape, w_rows.dtype),
            pltpu.VMEM((blocks, rows, keys), jnp.float32),
            pltpu.SemaphoreType.DMA((6,)),
        ],
        cost_estimate=pl.CostEstimate(
            flops=2 * blocks * rows * keys * channels, transcendentals=0, bytes_accessed=8000000
        ),
        compiler_params=pltpu.CompilerParams(vmem_limit_bytes=6 * 2**20),
        name="prepare",
    )(*(stay(a) for a in (pair, mask_row, w_rows, own, noise, w_qkv)))


def pack(ancestors, own, other, noise, bias):
    particles, rows, width = own.shape
    used = rows * (width // LANES)

    def kernel(anc_ref, own_ref, other_ref, noise_ref, bias_ref, out_ref):
        dom = lax.axis_index("dom")
        for p in range(particles):
            a = anc_ref[p]
            local = lax.rem(a, particles)
            mine = lax.div(a, particles) == dom
            value = jnp.where(mine, own_ref[local], other_ref[local])
            value = value.astype(jnp.float32) + 0.5 * noise_ref[p].astype(jnp.float32)
            value = value.astype(jnp.bfloat16)
            for k in range(width // LANES):
                out_ref[p, k * rows : (k + 1) * rows, :] = value[:, k * LANES : (k + 1) * LANES]
            out_ref[p, used:, :] = bias_ref[...]

    return pl.pallas_call(
        kernel,
        out_shape=jax.ShapeDtypeStruct((particles, used + bias.shape[0], LANES), jnp.bfloat16),
        in_specs=[in_smem()] + [whole_vmem()] * 4,
        out_specs=whole_vmem(),
        compiler_params=pltpu.CompilerParams(vmem_limit_bytes=6 * 2**20),
        name="pack",
    )(ancestors, own, other, noise, bias)


def across(left, right):
    return lax.dot_general(
        left, right, (((1,), (1,)), ((), ())), preferred_element_type=jnp.float32
    )


def project(normed, w_buf, q_ref, k_ref, v_ref, width, scale):
    q_ref[...] = (
        jnp.dot(normed, w_buf[:, :width], preferred_element_type=jnp.float32) * scale
    ).astype(jnp.bfloat16)
    k_ref[...] = jnp.dot(
        normed, w_buf[:, width : 2 * width], preferred_element_type=jnp.float32
    ).astype(jnp.bfloat16)
    v_ref[...] = jnp.dot(
        normed, w_buf[:, 2 * width :], preferred_element_type=jnp.float32
    ).astype(jnp.bfloat16)


def first_project(received, w_first, rows, width, scale):
    sources = received.shape[0]
    tokens = sources * rows

    def kernel(recv_ref, w_ref, x_ref, q_ref, k_ref, v_ref):
        for s in range(sources):
            for k in range(width // LANES):
                x_ref[s * rows : (s + 1) * rows, k * LANES : (k + 1) * LANES] = recv_ref[
                    s, k * rows : (k + 1) * rows, :
                ]
        normed = layer_norm(x_ref[...]).astype(jnp.bfloat16)
        project(normed, w_ref, q_ref, k_ref, v_ref, width, scale)

    shape = jax.ShapeDtypeStruct((tokens, width), jnp.bfloat16)
    return pl.pallas_call(
        kernel,
        out_shape=(shape,) * 4,
        in_specs=[whole_vmem(), whole_vmem()],
        out_specs=(whole_vmem(),) * 4,
        compiler_params=pltpu.CompilerParams(vmem_limit_bytes=12 * 2**20),
        cost_estimate=pl.CostEstimate(
            flops=6 * tokens * width * width, transcendentals=0, bytes_accessed=8 * width * width
        ),
        name="first_project",
    )(received, w_first)


def layers(mask, stream, query, keys, values, received, other, w_qkv, w_out, rows, heads, scale):
    tokens, width = stream.shape
    layer_count = w_qkv.shape[0]
    sources = received.shape[0]
    head_width = width // heads
    half = heads // 2
    stream_rows = rows * (width // LANES)

    def kernel(
        mask_ref, x_ref, q_in, k_in, v_in, recv_ref, other_ref, wq_hbm, wo_hbm,
        out_ref, x_buf, q_buf, k_buf, v_buf, vt_buf, at_buf, wq_buf, wo_buf, wq_sem, wo_sem,
    ):
        wo_copies = [
            pltpu.make_async_copy(wo_hbm.at[l], wo_buf.at[l], wo_sem.at[l])
            for l in range(layer_count)
        ]
        wq_copies = [
            pltpu.make_async_copy(wq_hbm.at[l], wq_buf.at[l - 1], wq_sem.at[l - 1])
            for l in range(1, layer_count)
        ]
        wo_copies[0].start()
        for l in range(1, layer_count):
            wq_copies[l - 1].start()
            wo_copies[l].start()
        is_first = lax.axis_index("dom") == 0
        anyone = jnp.max(mask_ref[...], axis=-1, keepdims=True)
        floor = jnp.where(anyone > 0, 0.0, MASKED).astype(jnp.float32)
        eye = jnp.where(
            lax.broadcasted_iota(jnp.int32, (tokens, tokens), 0)
            == lax.broadcasted_iota(jnp.int32, (tokens, tokens), 1),
            1.0, 0.0,
        ).astype(jnp.bfloat16)

        for l in range(layer_count):
            q_ref, k_ref, v_ref = (q_in, k_in, v_in) if l == 0 else (q_buf, k_buf, v_buf)
            stream_ref = x_ref if l == 0 else x_buf
            for t in range(0, width, LANES):
                vt_buf[t : t + LANES, :] = across(eye, v_ref[:, t : t + LANES]).astype(jnp.bfloat16)
            for h in range(heads):
                low = h * head_width
                high = low + head_width
                start = low // LANES * LANES
                stop = -(-high // LANES) * LANES
                lane = lax.broadcasted_iota(jnp.int32, (1, stop - start), 1) + start
                inside = jnp.where((lane >= low) & (lane < high), 1.0, 0.0).astype(jnp.bfloat16)
                base = stream_rows + (l * half + h % half) * rows
                near = recv_ref[:, base : base + rows, :].reshape(tokens, tokens)
                far = other_ref[:, base : base + rows, :].reshape(tokens, tokens)
                bias = jnp.where(is_first, near, far) if h < half else jnp.where(is_first, far, near)
                scores = across(
                    jnp.concatenate([k_ref[:, start:stop], eye], axis=1),
                    jnp.concatenate([q_ref[:, start:stop] * inside, bias], axis=1),
                ) + floor
                raised = jnp.exp(scores - jnp.max(scores, axis=0, keepdims=True))
                total = jnp.sum(raised, axis=0, keepdims=True)
                out = jnp.dot(
                    vt_buf[low:high, :], raised.astype(jnp.bfloat16),
                    preferred_element_type=jnp.float32,
                )
                at_buf[low:high, :] = (out * (1.0 / total)).astype(jnp.bfloat16)
            attended = across(eye, at_buf[...]).astype(jnp.bfloat16)
            wo_copies[l].wait()
            update = jnp.dot(attended, wo_buf[l], preferred_element_type=jnp.float32)
            moved = (stream_ref[...].astype(jnp.float32) + update).astype(jnp.bfloat16)
            if l + 1 < layer_count:
                x_buf[...] = moved
                normed = layer_norm(moved).astype(jnp.bfloat16)
                wq_copies[l].wait()
                project(normed, wq_buf.at[l], q_buf, k_buf, v_buf, width, scale)
            else:
                for s in range(sources):
                    out_ref[s] = moved[s * rows : (s + 1) * rows, :]

    wide = pltpu.VMEM((tokens, width), jnp.bfloat16)
    tall = pltpu.VMEM((width, tokens), jnp.bfloat16)
    return pl.pallas_call(
        kernel,
        out_shape=jax.ShapeDtypeStruct((sources, rows, width), jnp.bfloat16),
        in_specs=[whole_vmem()] * 7 + [in_hbm()] * 2,
        out_specs=whole_vmem(),
        scratch_shapes=[
            wide, wide, wide, wide, tall, tall,
            pltpu.VMEM((layer_count - 1, width, 3 * width), jnp.bfloat16),
            pltpu.VMEM((layer_count, width, width), jnp.bfloat16),
            pltpu.SemaphoreType.DMA((layer_count - 1,)),
            pltpu.SemaphoreType.DMA((layer_count,)),
        ],
        compiler_params=pltpu.CompilerParams(vmem_limit_bytes=20 * 2**20),
        cost_estimate=pl.CostEstimate(
            flops=14 * tokens * width * width, transcendentals=2 * heads * tokens * tokens,
            bytes_accessed=10 * width * width,
        ),
        name="layers",
    )(mask, stream, query, keys, values, received, other, stay(w_qkv), stay(w_out))


def spread_body(states, ancestors, noise, pair, token_mask, w_qkv, w_out, w_pair):
    particles, rows, width = states.shape
    heads = w_pair.shape[2]
    scale = (width // heads) ** (-0.5)
    swap = [(0, 1), (1, 0)]
    mask_row = token_mask.reshape(1, -1)
    other_states = lax.ppermute(states, "dom", swap)
    bias, own, local_noise, w_first = prepare(
        pair, mask_row, w_pair.transpose(0, 2, 1), states, noise, w_qkv
    )
    packed = pack(ancestors, own, other_states, local_noise, bias)
    received = lax.all_to_all(packed, "tok", 0, 0, tiled=True)
    other = lax.ppermute(received, "dom", swap)
    stream, query, keys, values = first_project(received, w_first, rows, width, scale)
    result = layers(
        mask_row, stream, query, keys, values, received, other, w_qkv, w_out, rows, heads, scale
    )
    return lax.all_to_all(result, "tok", 0, 0, tiled=True)


def solution(mesh):
    placed = (
        P(("groups", "dom"), "tok", None),
        P(("groups", "dom")),
        P(("groups", "dom"), "tok", None),
        P(("groups", "tok"), None, None),
        P("groups"),
        P(),
        P(),
        P(),
    )

    def body(states, ancestors, noise, pair, token_mask, w_qkv, w_out, w_pair):
        particles, rows, width = states.shape
        fits = (
            particles == mesh.shape["tok"]
            and mesh.shape["dom"] == 2
            and w_pair.shape[2] % 2 == 0
            and pair.shape[1] == LANES
            and pair.shape[2] == LANES
            and width % LANES == 0
            and rows % 16 == 0
            and (width // w_pair.shape[2]) % 16 == 0
        )
        chosen = spread_body if fits else gathered_body
        return chosen(states, ancestors, noise, pair, token_mask, w_qkv, w_out, w_pair)

    return jax.shard_map(
        body,
        mesh=mesh,
        in_specs=placed,
        out_specs=P(("groups", "dom"), "tok", None),
        check_vma=False,
    )
```

```python
import jax
import jax.numpy as jnp
from jax import lax
from jax.experimental import pallas as pl
from jax.experimental.pallas import tpu as pltpu
from jax.sharding import PartitionSpec as P

MASKED = -1000000000.0
LANES = 128


def layer_norm(stream):
    values = stream.astype(jnp.float32)
    average = jnp.mean(values, axis=-1, keepdims=True)
    centred = values - average
    spread = jnp.mean(centred * centred, axis=-1, keepdims=True)
    return centred * lax.rsqrt(spread + 1e-05)


def gathered_body(states, ancestors, noise, pair, token_mask, w_qkv, w_out, w_pair):
    part_count = states.shape[0]
    tok_rows = states.shape[1]
    model_width = states.shape[2]
    head_count = w_pair.shape[2]
    head_width = model_width // head_count
    layer_count = w_qkv.shape[0]
    total_keys = pair.shape[1]
    everyone = lax.all_gather(states, "dom", axis=0, tiled=True)
    chosen = jnp.take(everyone, ancestors, axis=0)
    stream = (chosen.astype(jnp.float32) + 0.5 * noise.astype(jnp.float32)).astype(jnp.bfloat16)
    penalty = jnp.where(token_mask > 0, 0.0, MASKED).astype(jnp.float32)
    pair_terms = jnp.einsum("ijc,lch->lhij", pair, w_pair, preferred_element_type=jnp.float32)
    full_bias = pair_terms + penalty[None, None, None, :]
    query_scale = head_width ** (-0.5)
    for layer_index in range(layer_count):
        normed = layer_norm(stream).astype(jnp.bfloat16)
        projected = jnp.dot(
            normed.reshape(part_count * tok_rows, model_width),
            w_qkv[layer_index],
            preferred_element_type=jnp.float32,
        )
        projected = projected.reshape(part_count, tok_rows, 3 * model_width)
        query = (projected[..., :model_width] * query_scale).astype(jnp.bfloat16)
        both = projected[..., model_width:].astype(jnp.bfloat16)
        query_heads = query.reshape(part_count, tok_rows, head_count, head_width)
        gathered = lax.all_gather(both, "tok", axis=1, tiled=True)
        all_keys, all_values = gathered[..., :model_width], gathered[..., model_width:]
        key_heads = all_keys.reshape(part_count, total_keys, head_count, head_width)
        scores = (
            jnp.einsum(
                "pihe,pjhe->phij", query_heads, key_heads, preferred_element_type=jnp.float32
            )
            + full_bias[layer_index][None]
        )
        weights = jax.nn.softmax(scores, axis=-1).astype(jnp.bfloat16)
        value_heads = all_values.reshape(part_count, total_keys, head_count, head_width)
        attended = jnp.einsum(
            "phij,pjhe->pihe", weights, value_heads, preferred_element_type=jnp.float32
        ).astype(jnp.bfloat16)
        attended = attended.reshape(part_count * tok_rows, model_width)
        update = jnp.dot(attended, w_out[layer_index], preferred_element_type=jnp.float32)
        update = update.reshape(part_count, tok_rows, model_width)
        stream = (stream.astype(jnp.float32) + update).astype(jnp.bfloat16)
    return stream


def whole_vmem():
    return pl.BlockSpec(memory_space=pltpu.VMEM)


def in_hbm():
    return pl.BlockSpec(memory_space=pltpu.HBM)


def stay(array):
    return pltpu.with_memory_space_constraint(array, pltpu.HBM)


def in_smem():
    return pl.BlockSpec(memory_space=pltpu.SMEM)


def prepare(pair, mask_row, w_rows, own, noise, w_qkv):
    rows, keys, channels = pair.shape
    layer_count, heads, _ = w_rows.shape
    half = heads // 2
    blocks = layer_count * half

    def kernel(
        pair_hbm, mask_hbm, w_hbm, own_hbm, noise_hbm, wq_hbm,
        bias_ref, own_ref, noise_ref, pair_ref, mask_ref, w_ref, rows_ref, sem,
    ):
        copies = [
            pltpu.make_async_copy(mask_hbm, mask_ref, sem.at[0]),
            pltpu.make_async_copy(w_hbm, w_ref, sem.at[1]),
            pltpu.make_async_copy(pair_hbm, pair_ref, sem.at[2]),
            pltpu.make_async_copy(own_hbm, own_ref, sem.at[3]),
            pltpu.make_async_copy(noise_hbm, noise_ref, sem.at[4]),
        ]
        for copy in copies:
            copy.start()
        copies[0].wait()
        copies[1].wait()
        penalty = jnp.where(mask_ref[...] > 0, 0.0, MASKED).astype(jnp.float32)
        is_first = lax.axis_index("dom") == 0
        sent = jnp.concatenate(
            [
                jnp.where(is_first, w[:half], w[half:])
                for w in (w_ref[l].astype(jnp.float32) for l in range(layer_count))
            ],
            axis=0,
        ).astype(jnp.bfloat16)
        copies[2].wait()
        for i in range(rows):
            piece = across(sent, pair_ref[i]) + penalty
            rows_ref[:, i, :] = piece - jnp.max(piece, axis=-1, keepdims=True)
        for h in range(blocks):
            bias_ref[h * rows : (h + 1) * rows, :] = rows_ref[h].astype(jnp.bfloat16)
        for copy in copies[3:]:
            copy.wait()

    return pl.pallas_call(
        kernel,
        out_shape=(
            jax.ShapeDtypeStruct((blocks * rows, keys), jnp.bfloat16),
            jax.ShapeDtypeStruct(own.shape, own.dtype),
            jax.ShapeDtypeStruct(noise.shape, noise.dtype),
        ),
        in_specs=[in_hbm()] * 6,
        out_specs=(whole_vmem(),) * 3,
        scratch_shapes=[
            pltpu.VMEM(pair.shape, pair.dtype),
            pltpu.VMEM(mask_row.shape, mask_row.dtype),
            pltpu.VMEM(w_rows.shape, w_rows.dtype),
            pltpu.VMEM((blocks, rows, keys), jnp.float32),
            pltpu.SemaphoreType.DMA((5,)),
        ],
        cost_estimate=pl.CostEstimate(
            flops=2 * blocks * rows * keys * channels, transcendentals=0, bytes_accessed=8000000
        ),
        compiler_params=pltpu.CompilerParams(vmem_limit_bytes=6 * 2**20),
        name="prepare",
    )(*(stay(a) for a in (pair, mask_row, w_rows, own, noise, w_qkv)))


def pack(ancestors, own, other, noise, bias):
    particles, rows, width = own.shape
    used = rows * (width // LANES)

    def kernel(anc_ref, own_ref, other_ref, noise_ref, bias_ref, out_ref):
        dom = lax.axis_index("dom")
        for p in range(particles):
            a = anc_ref[p]
            local = lax.rem(a, particles)
            mine = lax.div(a, particles) == dom
            value = jnp.where(mine, own_ref[local], other_ref[local])
            value = value.astype(jnp.float32) + 0.5 * noise_ref[p].astype(jnp.float32)
            value = value.astype(jnp.bfloat16)
            for k in range(width // LANES):
                out_ref[p, k * rows : (k + 1) * rows, :] = value[:, k * LANES : (k + 1) * LANES]
            out_ref[p, used:, :] = bias_ref[...]

    return pl.pallas_call(
        kernel,
        out_shape=jax.ShapeDtypeStruct((particles, used + bias.shape[0], LANES), jnp.bfloat16),
        in_specs=[in_smem()] + [whole_vmem()] * 4,
        out_specs=whole_vmem(),
        compiler_params=pltpu.CompilerParams(vmem_limit_bytes=6 * 2**20),
        name="pack",
    )(ancestors, own, other, noise, bias)


def across(left, right):
    return lax.dot_general(
        left, right, (((1,), (1,)), ((), ())), preferred_element_type=jnp.float32
    )


def identity(size):
    down = lax.broadcasted_iota(jnp.int32, (size, size), 0)
    along = lax.broadcasted_iota(jnp.int32, (size, size), 1)
    return jnp.where(down == along, 1.0, 0.0).astype(jnp.bfloat16)


def project(stream, w_ref, q_ref, k_ref, vt_ref, eye, scale):
    width = stream.shape[1]
    normed = layer_norm(stream).astype(jnp.bfloat16)
    q_ref[...] = (
        jnp.dot(normed, w_ref[:, :width], preferred_element_type=jnp.float32) * scale
    ).astype(jnp.bfloat16)
    k_ref[...] = jnp.dot(
        normed, w_ref[:, width : 2 * width], preferred_element_type=jnp.float32
    ).astype(jnp.bfloat16)
    values = jnp.dot(
        normed, w_ref[:, 2 * width :], preferred_element_type=jnp.float32
    ).astype(jnp.bfloat16)
    for t in range(0, width, LANES):
        vt_ref[t : t + LANES, :] = across(eye, values[:, t : t + LANES]).astype(jnp.bfloat16)


def attend(groups, first_row, rows, head_width, q_ref, k_ref, vt_ref, at_ref, work, eye, floor):
    s_buf, e_buf, n_buf = work
    tokens = eye.shape[0]
    half = q_ref.shape[1] // head_width // 2
    every = [(g * half + h, h, base, bias) for g, (base, bias) in enumerate(groups) for h in range(half)]
    for slot, h, base, bias_ref in every:
        low = h * head_width
        high = low + head_width
        start = low // LANES * LANES
        stop = -(-high // LANES) * LANES
        lane = lax.broadcasted_iota(jnp.int32, (1, stop - start), 1) + start
        inside = jnp.where((lane >= low) & (lane < high), 1.0, 0.0).astype(jnp.bfloat16)
        cols = pl.ds(pl.multiple_of(base + start, LANES), stop - start)
        at = first_row + h * rows
        bias = bias_ref[:, at : at + rows, :].reshape(tokens, tokens)
        s_buf[slot] = across(
            jnp.concatenate([k_ref[:, cols], eye], axis=1),
            jnp.concatenate([q_ref[:, cols] * inside, bias], axis=1),
        )
    for slot, h, base, bias_ref in every:
        scores = s_buf[slot] + floor
        raised = jnp.exp(scores - jnp.max(scores, axis=0, keepdims=True))
        n_buf[slot : slot + 1, :] = 1.0 / jnp.sum(raised, axis=0, keepdims=True)
        e_buf[slot] = raised.astype(jnp.bfloat16)
    for slot, h, base, bias_ref in every:
        own = pl.ds(pl.multiple_of(base + h * head_width, 16), head_width)
        out = jnp.dot(vt_ref[own, :], e_buf[slot], preferred_element_type=jnp.float32)
        at_ref[own, :] = (out * n_buf[slot : slot + 1, :]).astype(jnp.bfloat16)


def row_floor(mask_ref):
    anyone = jnp.max(mask_ref[...], axis=-1, keepdims=True)
    return jnp.where(anyone > 0, 0.0, MASKED).astype(jnp.float32)


def work_space(slots, tokens):
    return [
        pltpu.VMEM((slots, tokens, tokens), jnp.float32),
        pltpu.VMEM((slots, tokens, tokens), jnp.bfloat16),
        pltpu.VMEM((slots, tokens), jnp.float32),
    ]


def first_half(mask, received, w_qkv, rows, heads, scale):
    sources = received.shape[0]
    tokens = sources * rows
    width = w_qkv.shape[1]
    stream_rows = rows * (width // LANES)

    def kernel(mask_ref, recv_ref, w_ref, x_ref, q_ref, k_ref, vt_ref, at_ref, *work):
        for s in range(sources):
            for k in range(width // LANES):
                x_ref[s * rows : (s + 1) * rows, k * LANES : (k + 1) * LANES] = recv_ref[
                    s, k * rows : (k + 1) * rows, :
                ]
        eye = identity(tokens)
        project(x_ref[...], w_ref.at[0], q_ref, k_ref, vt_ref, eye, scale)
        near = lax.axis_index("dom") * (width // 2)
        attend(
            [(near, recv_ref)], stream_rows, rows, width // heads,
            q_ref, k_ref, vt_ref, at_ref, work, eye, row_floor(mask_ref),
        )

    wide = jax.ShapeDtypeStruct((tokens, width), jnp.bfloat16)
    tall = jax.ShapeDtypeStruct((width, tokens), jnp.bfloat16)
    return pl.pallas_call(
        kernel,
        out_shape=(wide, wide, wide, tall, tall),
        in_specs=[whole_vmem()] * 3,
        out_specs=(whole_vmem(),) * 5,
        scratch_shapes=work_space(heads // 2, tokens),
        compiler_params=pltpu.CompilerParams(vmem_limit_bytes=8 * 2**20),
        cost_estimate=pl.CostEstimate(
            flops=6 * tokens * width * width, transcendentals=heads * tokens * tokens // 2,
            bytes_accessed=8 * width * width,
        ),
        name="first_half",
    )(mask, received, w_qkv)


def layers(mask, stream, query, keys, values, attended, received, other, w_qkv, w_out, rows, heads, scale):
    tokens, width = stream.shape
    layer_count = w_qkv.shape[0]
    sources = received.shape[0]
    half = heads // 2
    stream_rows = rows * (width // LANES)

    def kernel(
        mask_ref, x_ref, q_in, k_in, vt_in, at_in, recv_ref, other_ref, wq_ref, wo_ref,
        out_ref, x_buf, q_buf, k_buf, vt_buf, at_buf, *work,
    ):
        here = lax.axis_index("dom")
        near = here * (width // 2)
        far = (1 - here) * (width // 2)
        floor = row_floor(mask_ref)
        eye = identity(tokens)
        ready = pl.ds(pl.multiple_of(near, LANES), width // 2)
        at_buf[ready, :] = at_in[ready, :]

        for l in range(layer_count):
            q_ref, k_ref, vt_ref = (q_in, k_in, vt_in) if l == 0 else (q_buf, k_buf, vt_buf)
            stream_ref = x_ref if l == 0 else x_buf
            groups = [(far, other_ref)] if l == 0 else [(near, recv_ref), (far, other_ref)]
            attend(
                groups, stream_rows + l * half * rows, rows, width // heads,
                q_ref, k_ref, vt_ref, at_buf, work, eye, floor,
            )
            together = across(eye, at_buf[...]).astype(jnp.bfloat16)
            update = jnp.dot(together, wo_ref[l], preferred_element_type=jnp.float32)
            moved = (stream_ref[...].astype(jnp.float32) + update).astype(jnp.bfloat16)
            if l + 1 < layer_count:
                x_buf[...] = moved
                project(moved, wq_ref.at[l + 1], q_buf, k_buf, vt_buf, eye, scale)
            else:
                for s in range(sources):
                    out_ref[s] = moved[s * rows : (s + 1) * rows, :]

    wide = pltpu.VMEM((tokens, width), jnp.bfloat16)
    tall = pltpu.VMEM((width, tokens), jnp.bfloat16)
    return pl.pallas_call(
        kernel,
        out_shape=jax.ShapeDtypeStruct((sources, rows, width), jnp.bfloat16),
        in_specs=[whole_vmem()] * 10,
        out_specs=whole_vmem(),
        scratch_shapes=[
            wide, wide, wide, tall, tall,
        ] + work_space(heads, tokens),
        compiler_params=pltpu.CompilerParams(vmem_limit_bytes=8 * 2**20),
        cost_estimate=pl.CostEstimate(
            flops=14 * tokens * width * width, transcendentals=2 * heads * tokens * tokens,
            bytes_accessed=10 * width * width,
        ),
        name="layers",
    )(mask, stream, query, keys, values, attended, received, other, w_qkv, w_out)


def spread_body(states, ancestors, noise, pair, token_mask, w_qkv, w_out, w_pair):
    particles, rows, width = states.shape
    heads = w_pair.shape[2]
    scale = (width // heads) ** (-0.5)
    swap = [(0, 1), (1, 0)]
    mask_row = token_mask.reshape(1, -1)
    other_states = lax.ppermute(states, "dom", swap)
    bias, own, local_noise = prepare(
        pair, mask_row, w_pair.transpose(0, 2, 1), states, noise, w_qkv
    )
    packed = pack(ancestors, own, other_states, local_noise, bias)
    received = lax.all_to_all(packed, "tok", 0, 0, tiled=True)
    other = lax.ppermute(received, "dom", swap)
    state = first_half(mask_row, received, w_qkv, rows, heads, scale)
    result = layers(mask_row, *state, received, other, w_qkv, w_out, rows, heads, scale)
    return lax.all_to_all(result, "tok", 0, 0, tiled=True)


def solution(mesh):
    placed = (
        P(("groups", "dom"), "tok", None),
        P(("groups", "dom")),
        P(("groups", "dom"), "tok", None),
        P(("groups", "tok"), None, None),
        P("groups"),
        P(),
        P(),
        P(),
    )

    def body(states, ancestors, noise, pair, token_mask, w_qkv, w_out, w_pair):
        particles, rows, width = states.shape
        fits = (
            particles == mesh.shape["tok"]
            and mesh.shape["dom"] == 2
            and width % (2 * LANES) == 0
            and pair.shape[1] == LANES
            and pair.shape[2] == LANES
            and rows % 16 == 0
            and (width // w_pair.shape[2]) % 16 == 0
        )
        chosen = spread_body if fits else gathered_body
        return chosen(states, ancestors, noise, pair, token_mask, w_qkv, w_out, w_pair)

    return jax.shard_map(
        body,
        mesh=mesh,
        in_specs=placed,
        out_specs=P(("groups", "dom"), "tok", None),
        check_vma=False,
    )
```

```python
import jax
import jax.numpy as jnp
from jax import lax
from jax.experimental import pallas as pl
from jax.experimental.pallas import tpu as pltpu
from jax.sharding import PartitionSpec as P

MASKED = -1000000000.0
LANES = 128


def layer_norm(stream):
    values = stream.astype(jnp.float32)
    average = jnp.mean(values, axis=-1, keepdims=True)
    centred = values - average
    spread = jnp.mean(centred * centred, axis=-1, keepdims=True)
    return centred * lax.rsqrt(spread + 1e-05)


def gathered_body(states, ancestors, noise, pair, token_mask, w_qkv, w_out, w_pair):
    part_count = states.shape[0]
    tok_rows = states.shape[1]
    model_width = states.shape[2]
    head_count = w_pair.shape[2]
    head_width = model_width // head_count
    layer_count = w_qkv.shape[0]
    total_keys = pair.shape[1]
    everyone = lax.all_gather(states, "dom", axis=0, tiled=True)
    chosen = jnp.take(everyone, ancestors, axis=0)
    stream = (chosen.astype(jnp.float32) + 0.5 * noise.astype(jnp.float32)).astype(jnp.bfloat16)
    penalty = jnp.where(token_mask > 0, 0.0, MASKED).astype(jnp.float32)
    pair_terms = jnp.einsum("ijc,lch->lhij", pair, w_pair, preferred_element_type=jnp.float32)
    full_bias = pair_terms + penalty[None, None, None, :]
    query_scale = head_width ** (-0.5)
    for layer_index in range(layer_count):
        normed = layer_norm(stream).astype(jnp.bfloat16)
        projected = jnp.dot(
            normed.reshape(part_count * tok_rows, model_width),
            w_qkv[layer_index],
            preferred_element_type=jnp.float32,
        )
        projected = projected.reshape(part_count, tok_rows, 3 * model_width)
        query = (projected[..., :model_width] * query_scale).astype(jnp.bfloat16)
        both = projected[..., model_width:].astype(jnp.bfloat16)
        query_heads = query.reshape(part_count, tok_rows, head_count, head_width)
        gathered = lax.all_gather(both, "tok", axis=1, tiled=True)
        all_keys, all_values = gathered[..., :model_width], gathered[..., model_width:]
        key_heads = all_keys.reshape(part_count, total_keys, head_count, head_width)
        scores = (
            jnp.einsum(
                "pihe,pjhe->phij", query_heads, key_heads, preferred_element_type=jnp.float32
            )
            + full_bias[layer_index][None]
        )
        weights = jax.nn.softmax(scores, axis=-1).astype(jnp.bfloat16)
        value_heads = all_values.reshape(part_count, total_keys, head_count, head_width)
        attended = jnp.einsum(
            "phij,pjhe->pihe", weights, value_heads, preferred_element_type=jnp.float32
        ).astype(jnp.bfloat16)
        attended = attended.reshape(part_count * tok_rows, model_width)
        update = jnp.dot(attended, w_out[layer_index], preferred_element_type=jnp.float32)
        update = update.reshape(part_count, tok_rows, model_width)
        stream = (stream.astype(jnp.float32) + update).astype(jnp.bfloat16)
    return stream


def whole_vmem():
    return pl.BlockSpec(memory_space=pltpu.VMEM)


def in_hbm():
    return pl.BlockSpec(memory_space=pltpu.HBM)


def stay(array):
    return pltpu.with_memory_space_constraint(array, pltpu.HBM)


def in_smem():
    return pl.BlockSpec(memory_space=pltpu.SMEM)


def prepare(pair, mask_row, w_rows, own, noise, w_qkv):
    rows, keys, channels = pair.shape
    blocks = w_rows.shape[0]

    def kernel(
        pair_hbm, mask_hbm, w_hbm, own_hbm, noise_hbm, wq_hbm,
        bias_ref, own_ref, noise_ref, pair_ref, mask_ref, w_ref, rows_ref, sem,
    ):
        copies = [
            pltpu.make_async_copy(mask_hbm, mask_ref, sem.at[0]),
            pltpu.make_async_copy(w_hbm, w_ref, sem.at[1]),
            pltpu.make_async_copy(pair_hbm, pair_ref, sem.at[2]),
            pltpu.make_async_copy(own_hbm, own_ref, sem.at[3]),
            pltpu.make_async_copy(noise_hbm, noise_ref, sem.at[4]),
        ]
        for copy in copies:
            copy.start()
        copies[0].wait()
        copies[1].wait()
        penalty = jnp.where(mask_ref[...] > 0, 0.0, MASKED).astype(jnp.float32)
        copies[2].wait()
        for i in range(rows):
            piece = across(w_ref[...], pair_ref[i]) + penalty
            rows_ref[:, i, :] = piece - jnp.max(piece, axis=-1, keepdims=True)
        for h in range(blocks):
            bias_ref[h * rows : (h + 1) * rows, :] = rows_ref[h].astype(jnp.bfloat16)
        for copy in copies[3:]:
            copy.wait()

    return pl.pallas_call(
        kernel,
        out_shape=(
            jax.ShapeDtypeStruct((blocks * rows, keys), jnp.bfloat16),
            jax.ShapeDtypeStruct(own.shape, own.dtype),
            jax.ShapeDtypeStruct(noise.shape, noise.dtype),
        ),
        in_specs=[in_hbm()] * 6,
        out_specs=(whole_vmem(),) * 3,
        scratch_shapes=[
            pltpu.VMEM(pair.shape, pair.dtype),
            pltpu.VMEM(mask_row.shape, mask_row.dtype),
            pltpu.VMEM(w_rows.shape, w_rows.dtype),
            pltpu.VMEM((blocks, rows, keys), jnp.float32),
            pltpu.SemaphoreType.DMA((5,)),
        ],
        cost_estimate=pl.CostEstimate(
            flops=2 * blocks * rows * keys * channels, transcendentals=0, bytes_accessed=8000000
        ),
        compiler_params=pltpu.CompilerParams(vmem_limit_bytes=6 * 2**20),
        name="prepare",
    )(*(stay(a) for a in (pair, mask_row, w_rows, own, noise, w_qkv)))


def block_source(position):
    here, dom = lax.axis_index("tok"), lax.axis_index("dom")
    if position < 2:
        return jnp.bitwise_xor(here, position)
    return jnp.bitwise_xor(here, position + dom if position % 2 == 0 else position - dom)


def pack(ancestors, other_ancestors, own, other, noise, other_noise, bias):
    particles, rows, width = own.shape
    used = rows * (width // LANES)
    total = bias.shape[0]
    served = [0, 1] + list(range(2, particles, 2))

    def kernel(anc_ref, far_anc_ref, own_ref, other_ref, noise_ref, far_noise_ref, bias_ref, *outs):
        dom = lax.axis_index("dom")

        def put(out_ref, first, ancestor, noise_block):
            local = lax.rem(ancestor, particles)
            mine = lax.div(ancestor, particles) == dom
            value = jnp.where(mine, own_ref[local], other_ref[local])
            value = value.astype(jnp.float32) + 0.5 * noise_block.astype(jnp.float32)
            value = value.astype(jnp.bfloat16)
            for k in range(width // LANES):
                out_ref[first + k * rows : first + (k + 1) * rows, :] = value[
                    :, k * LANES : (k + 1) * LANES
                ]

        for position, out_ref in zip(served, outs):
            target = block_source(position)
            put(out_ref, 0, anc_ref[target], noise_ref[target])
            out_ref[used : used + total, :] = bias_ref[...]
            if position > 1:
                put(out_ref, used + total, far_anc_ref[target], far_noise_ref[target])

    return pl.pallas_call(
        kernel,
        out_shape=tuple(
            jax.ShapeDtypeStruct((total + used * (1 if p < 2 else 2), LANES), own.dtype)
            for p in served
        ),
        in_specs=[in_smem()] * 2 + [whole_vmem()] * 5,
        out_specs=(whole_vmem(),) * len(served),
        compiler_params=pltpu.CompilerParams(vmem_limit_bytes=6 * 2**20),
        name="pack",
    )(ancestors, other_ancestors, own, other, noise, other_noise, bias)


def across(left, right):
    return lax.dot_general(
        left, right, (((1,), (1,)), ((), ())), preferred_element_type=jnp.float32
    )


def identity(size):
    down = lax.broadcasted_iota(jnp.int32, (size, size), 0)
    along = lax.broadcasted_iota(jnp.int32, (size, size), 1)
    return jnp.where(down == along, 1.0, 0.0).astype(jnp.bfloat16)


def block_rows(position, rows):
    return pl.ds(pl.multiple_of(block_source(position) * rows, rows), rows)


def project(stream, w_ref, q_ref, k_ref, vt_ref, n_ref, eye, scale, rows):
    tokens, width = stream.shape
    normed = layer_norm(stream).astype(jnp.bfloat16)
    n_ref[...] = (
        jnp.dot(normed, w_ref[:, :width], preferred_element_type=jnp.float32) * scale
    ).astype(jnp.bfloat16)
    k_ref[...] = jnp.dot(
        normed, w_ref[:, width : 2 * width], preferred_element_type=jnp.float32
    ).astype(jnp.bfloat16)
    values = jnp.dot(
        normed, w_ref[:, 2 * width :], preferred_element_type=jnp.float32
    ).astype(jnp.bfloat16)
    for t in range(0, width, LANES):
        vt_ref[t : t + LANES, :] = across(eye, values[:, t : t + LANES]).astype(jnp.bfloat16)
    for p in range(tokens // rows):
        q_ref[p * rows : (p + 1) * rows, :] = n_ref[block_rows(p, rows), :]


def attend(blocks, first_row, rows, head_width, q_ref, k_ref, vt_ref, at_ref, work, eye, floor):
    s_buf, e_buf, n_buf = work
    heads = q_ref.shape[1] // head_width
    for h in range(heads):
        low = h * head_width
        high = low + head_width
        start = low // LANES * LANES
        stop = -(-high // LANES) * LANES
        lane = lax.broadcasted_iota(jnp.int32, (1, stop - start), 1) + start
        inside = jnp.where((lane >= low) & (lane < high), 1.0, 0.0).astype(jnp.bfloat16)
        at = first_row + h * rows
        bias = jnp.concatenate([block[at : at + rows, :] for block in blocks], axis=0)
        s_buf[h] = across(
            jnp.concatenate([k_ref[:, start:stop], eye], axis=1),
            jnp.concatenate([q_ref[:, start:stop] * inside, bias], axis=1),
        )
    for h in range(heads):
        scores = s_buf[h] + floor
        raised = jnp.exp(scores - jnp.max(scores, axis=0, keepdims=True))
        n_buf[h : h + 1, :] = 1.0 / jnp.sum(raised, axis=0, keepdims=True)
        e_buf[h] = raised.astype(jnp.bfloat16)
    for h in range(heads):
        own = slice(h * head_width, (h + 1) * head_width)
        out = jnp.dot(vt_ref[own, :], e_buf[h], preferred_element_type=jnp.float32)
        at_ref[own, :] = (out * n_buf[h : h + 1, :]).astype(jnp.bfloat16)


def row_floor(mask_ref):
    anyone = jnp.max(mask_ref[...], axis=-1, keepdims=True)
    return jnp.where(anyone > 0, 0.0, MASKED).astype(jnp.float32)


def work_space(slots, tokens):
    return [
        pltpu.VMEM((slots, tokens, tokens), jnp.float32),
        pltpu.VMEM((slots, tokens, tokens), jnp.bfloat16),
        pltpu.VMEM((slots, tokens), jnp.float32),
    ]


def first_project(blocks, w_qkv, rows, bias_rows, scale):
    sources = len(blocks)
    width = w_qkv.shape[1]
    tokens = sources * rows

    def kernel(w_ref, *refs):
        blocks, (x_ref, q_ref, k_ref, vt_ref, n_ref) = refs[:sources], refs[sources:]
        for p in range(sources):
            first = 0 if p < 2 or p % 2 == 0 else rows * (width // LANES) + bias_rows
            for k in range(width // LANES):
                x_ref[block_rows(p, rows), k * LANES : (k + 1) * LANES] = blocks[p][
                    first + k * rows : first + (k + 1) * rows, :
                ]
        project(
            x_ref[...], w_ref.at[0], q_ref, k_ref, vt_ref, n_ref, identity(tokens), scale, rows
        )

    wide = jax.ShapeDtypeStruct((tokens, width), jnp.bfloat16)
    return pl.pallas_call(
        kernel,
        out_shape=(wide, wide, wide, jax.ShapeDtypeStruct((width, tokens), jnp.bfloat16)),
        in_specs=[whole_vmem()] * (1 + sources),
        out_specs=(whole_vmem(),) * 4,
        scratch_shapes=[pltpu.VMEM((tokens, width), jnp.bfloat16)],
        compiler_params=pltpu.CompilerParams(vmem_limit_bytes=8 * 2**20),
        cost_estimate=pl.CostEstimate(
            flops=6 * tokens * width * width, transcendentals=0, bytes_accessed=8 * width * width
        ),
        name="first_project",
    )(w_qkv, *blocks)


def layers(mask, stream, query, keys, values, blocks, w_qkv, w_out, heads, scale):
    tokens, width = stream.shape
    sources = len(blocks)
    rows = tokens // sources
    layer_count = w_qkv.shape[0]

    def kernel(mask_ref, x_ref, q_in, k_in, vt_in, wq_ref, wo_ref, *refs):
        bias_refs, refs = refs[:sources], refs[sources:]
        out_ref, x_buf, q_buf, k_buf, vt_buf, at_buf, n_buf, *work = refs
        floor = row_floor(mask_ref)
        eye = identity(tokens)
        for l in range(layer_count):
            q_ref, k_ref, vt_ref = (q_in, k_in, vt_in) if l == 0 else (q_buf, k_buf, vt_buf)
            attend(
                bias_refs, (width // LANES + l * heads) * rows, rows, width // heads,
                q_ref, k_ref, vt_ref, at_buf, work, eye, floor,
            )
            together = across(eye, at_buf[...]).astype(jnp.bfloat16)
            for p in range(sources):
                n_buf[block_rows(p, rows), :] = together[p * rows : (p + 1) * rows, :]
            update = jnp.dot(n_buf[...], wo_ref[l], preferred_element_type=jnp.float32)
            before = x_ref[...] if l == 0 else x_buf[...]
            moved = (before.astype(jnp.float32) + update).astype(jnp.bfloat16)
            if l + 1 < layer_count:
                x_buf[...] = moved
                project(
                    moved, wq_ref.at[l + 1], q_buf, k_buf, vt_buf, n_buf, eye, scale, rows
                )
            else:
                for s in range(sources):
                    out_ref[s] = moved[s * rows : (s + 1) * rows, :]

    wide = pltpu.VMEM((tokens, width), jnp.bfloat16)
    tall = pltpu.VMEM((width, tokens), jnp.bfloat16)
    return pl.pallas_call(
        kernel,
        out_shape=jax.ShapeDtypeStruct((sources, rows, width), jnp.bfloat16),
        in_specs=[whole_vmem()] * (7 + sources),
        out_specs=whole_vmem(),
        scratch_shapes=[wide, wide, wide, tall, tall, wide] + work_space(heads, tokens),
        compiler_params=pltpu.CompilerParams(vmem_limit_bytes=8 * 2**20),
        cost_estimate=pl.CostEstimate(
            flops=14 * tokens * width * width, transcendentals=2 * heads * tokens * tokens,
            bytes_accessed=10 * width * width,
        ),
        name="layers",
    )(mask, stream, query, keys, values, w_qkv, w_out, *blocks)


def spread_body(states, ancestors, noise, pair, token_mask, w_qkv, w_out, w_pair):
    particles, rows, width = states.shape
    layer_count, channels, heads = w_pair.shape
    scale = (width // heads) ** (-0.5)
    swap = [(0, 1), (1, 0)]
    mask_row = token_mask.reshape(1, -1)
    other_states = lax.ppermute(states, "dom", swap)
    other_noise = lax.ppermute(noise, "dom", swap)
    other_ancestors = lax.ppermute(ancestors, "dom", swap)
    bias, own, local_noise = prepare(
        pair, mask_row, w_pair.transpose(0, 2, 1).reshape(layer_count * heads, channels),
        states, noise, w_qkv,
    )
    kept, beside, *sent = pack(
        ancestors, other_ancestors, own, other_states, local_noise, other_noise, bias
    )
    beside = lax.ppermute(beside, "tok", [(t, t ^ 1) for t in range(particles)])
    blocks = []
    for k, block in reversed(list(zip(range(2, particles, 2), sent))):
        brought = lax.ppermute(
            block, ("tok", "dom"),
            [(2 * t + d, 2 * (t ^ (k + d)) + d) for t in range(particles) for d in range(2)],
        )
        if not blocks:
            brought, beside = lax.optimization_barrier((brought, beside))
        blocks = [brought, lax.ppermute(brought, "dom", swap)] + blocks
    blocks = [kept, beside] + blocks
    state = first_project(blocks, w_qkv, rows, bias.shape[0], scale)
    result = layers(mask_row, *state, blocks, w_qkv, w_out, heads, scale)
    return lax.all_to_all(result, "tok", 0, 0, tiled=True)


def solution(mesh):
    placed = (
        P(("groups", "dom"), "tok", None),
        P(("groups", "dom")),
        P(("groups", "dom"), "tok", None),
        P(("groups", "tok"), None, None),
        P("groups"),
        P(),
        P(),
        P(),
    )

    def body(states, ancestors, noise, pair, token_mask, w_qkv, w_out, w_pair):
        particles, rows, width = states.shape
        fits = (
            particles == mesh.shape["tok"]
            and particles & (particles - 1) == 0
            and particles > 2
            and mesh.shape["dom"] == 2
            and width % LANES == 0
            and pair.shape[1] == LANES
            and pair.shape[2] == LANES
            and rows % 16 == 0
            and (width // w_pair.shape[2]) % 16 == 0
        )
        chosen = spread_body if fits else gathered_body
        return chosen(states, ancestors, noise, pair, token_mask, w_qkv, w_out, w_pair)

    return jax.shard_map(
        body,
        mesh=mesh,
        in_specs=placed,
        out_specs=P(("groups", "dom"), "tok", None),
        check_vma=False,
    )
```

```python
import jax
import jax.numpy as jnp
from jax import lax
from jax.experimental import pallas as pl
from jax.experimental.pallas import tpu as pltpu
from jax.sharding import PartitionSpec as P

MASKED = -1000000000.0
LANES = 128


def layer_norm(stream):
    values = stream.astype(jnp.float32)
    average = jnp.mean(values, axis=-1, keepdims=True)
    centred = values - average
    spread = jnp.mean(centred * centred, axis=-1, keepdims=True)
    return centred * lax.rsqrt(spread + 1e-05)


def gathered_body(states, ancestors, noise, pair, token_mask, w_qkv, w_out, w_pair):
    part_count = states.shape[0]
    tok_rows = states.shape[1]
    model_width = states.shape[2]
    head_count = w_pair.shape[2]
    head_width = model_width // head_count
    layer_count = w_qkv.shape[0]
    total_keys = pair.shape[1]
    everyone = lax.all_gather(states, "dom", axis=0, tiled=True)
    chosen = jnp.take(everyone, ancestors, axis=0)
    stream = (chosen.astype(jnp.float32) + 0.5 * noise.astype(jnp.float32)).astype(jnp.bfloat16)
    penalty = jnp.where(token_mask > 0, 0.0, MASKED).astype(jnp.float32)
    pair_terms = jnp.einsum("ijc,lch->lhij", pair, w_pair, preferred_element_type=jnp.float32)
    full_bias = pair_terms + penalty[None, None, None, :]
    query_scale = head_width ** (-0.5)
    for layer_index in range(layer_count):
        normed = layer_norm(stream).astype(jnp.bfloat16)
        projected = jnp.dot(
            normed.reshape(part_count * tok_rows, model_width),
            w_qkv[layer_index],
            preferred_element_type=jnp.float32,
        )
        projected = projected.reshape(part_count, tok_rows, 3 * model_width)
        query = (projected[..., :model_width] * query_scale).astype(jnp.bfloat16)
        both = projected[..., model_width:].astype(jnp.bfloat16)
        query_heads = query.reshape(part_count, tok_rows, head_count, head_width)
        gathered = lax.all_gather(both, "tok", axis=1, tiled=True)
        all_keys, all_values = gathered[..., :model_width], gathered[..., model_width:]
        key_heads = all_keys.reshape(part_count, total_keys, head_count, head_width)
        scores = (
            jnp.einsum(
                "pihe,pjhe->phij", query_heads, key_heads, preferred_element_type=jnp.float32
            )
            + full_bias[layer_index][None]
        )
        weights = jax.nn.softmax(scores, axis=-1).astype(jnp.bfloat16)
        value_heads = all_values.reshape(part_count, total_keys, head_count, head_width)
        attended = jnp.einsum(
            "phij,pjhe->pihe", weights, value_heads, preferred_element_type=jnp.float32
        ).astype(jnp.bfloat16)
        attended = attended.reshape(part_count * tok_rows, model_width)
        update = jnp.dot(attended, w_out[layer_index], preferred_element_type=jnp.float32)
        update = update.reshape(part_count, tok_rows, model_width)
        stream = (stream.astype(jnp.float32) + update).astype(jnp.bfloat16)
    return stream


def whole_vmem():
    return pl.BlockSpec(memory_space=pltpu.VMEM)


def in_hbm():
    return pl.BlockSpec(memory_space=pltpu.HBM)


def stay(array):
    return pltpu.with_memory_space_constraint(array, pltpu.HBM)


def in_smem():
    return pl.BlockSpec(memory_space=pltpu.SMEM)


def prepare(pair, mask_row, w_rows, own, noise, w_qkv):
    rows, keys, channels = pair.shape
    layer_count, heads, _ = w_rows.shape
    half = heads // 2
    blocks = layer_count * heads

    def kernel(
        pair_hbm, mask_hbm, w_hbm, own_hbm, noise_hbm, wq_hbm,
        near_ref, far_ref, own_ref, noise_ref, pair_ref, mask_ref, w_ref, rows_ref, sem,
    ):
        copies = [
            pltpu.make_async_copy(mask_hbm, mask_ref, sem.at[0]),
            pltpu.make_async_copy(w_hbm, w_ref, sem.at[1]),
            pltpu.make_async_copy(pair_hbm, pair_ref, sem.at[2]),
            pltpu.make_async_copy(own_hbm, own_ref, sem.at[3]),
            pltpu.make_async_copy(noise_hbm, noise_ref, sem.at[4]),
        ]
        for copy in copies:
            copy.start()
        copies[0].wait()
        copies[1].wait()
        penalty = jnp.where(mask_ref[...] > 0, 0.0, MASKED).astype(jnp.float32)
        w_all = w_ref[...].reshape(blocks, channels)
        copies[2].wait()
        for i in range(rows):
            piece = across(w_all, pair_ref[i]) + penalty
            rows_ref[:, i, :] = piece - jnp.max(piece, axis=-1, keepdims=True)
        dom = lax.axis_index("dom")
        for l in range(layer_count):
            for h in range(half):
                at = (l * half + h) * rows
                near = l * heads + dom * half + h
                far = l * heads + (1 - dom) * half + h
                near_ref[at : at + rows, :] = rows_ref[near].astype(jnp.bfloat16)
                far_ref[at : at + rows, :] = rows_ref[far].astype(jnp.bfloat16)
        for copy in copies[3:]:
            copy.wait()

    part = jax.ShapeDtypeStruct((blocks // 2 * rows, keys), jnp.bfloat16)
    return pl.pallas_call(
        kernel,
        out_shape=(
            part, part,
            jax.ShapeDtypeStruct(own.shape, own.dtype),
            jax.ShapeDtypeStruct(noise.shape, noise.dtype),
        ),
        in_specs=[in_hbm()] * 6,
        out_specs=(whole_vmem(),) * 4,
        scratch_shapes=[
            pltpu.VMEM(pair.shape, pair.dtype),
            pltpu.VMEM(mask_row.shape, mask_row.dtype),
            pltpu.VMEM(w_rows.shape, w_rows.dtype),
            pltpu.VMEM((blocks, rows, keys), jnp.float32),
            pltpu.SemaphoreType.DMA((5,)),
        ],
        cost_estimate=pl.CostEstimate(
            flops=2 * blocks * rows * keys * channels, transcendentals=0, bytes_accessed=8000000
        ),
        compiler_params=pltpu.CompilerParams(vmem_limit_bytes=6 * 2**20),
        name="prepare",
    )(*(stay(a) for a in (pair, mask_row, w_rows, own, noise, w_qkv)))


def block_source(position):
    return jnp.bitwise_xor(lax.axis_index("tok"), position)


def pack(ancestors, own, other, noise, bias):
    particles, rows, width = own.shape
    used = rows * (width // LANES)
    total = bias.shape[0]
    served = [0, 1] + list(range(2, particles, 2))

    def kernel(anc_ref, own_ref, other_ref, noise_ref, bias_ref, *outs):
        dom = lax.axis_index("dom")

        def put(out_ref, first, particle):
            ancestor = anc_ref[particle]
            local = lax.rem(ancestor, particles)
            mine = lax.div(ancestor, particles) == dom
            value = jnp.where(mine, own_ref[local], other_ref[local])
            value = value.astype(jnp.float32) + 0.5 * noise_ref[particle].astype(jnp.float32)
            value = value.astype(jnp.bfloat16)
            for k in range(width // LANES):
                out_ref[first + k * rows : first + (k + 1) * rows, :] = value[
                    :, k * LANES : (k + 1) * LANES
                ]

        for position, out_ref in zip(served, outs):
            put(out_ref, 0, block_source(position))
            if position > 0:
                out_ref[used : used + total, :] = bias_ref[...]
            if position > 1:
                put(out_ref, used + total, block_source(position + 1))

    lengths = [used, used + total] + [total + 2 * used] * (len(served) - 2)
    return pl.pallas_call(
        kernel,
        out_shape=tuple(jax.ShapeDtypeStruct((length, LANES), own.dtype) for length in lengths),
        in_specs=[in_smem()] + [whole_vmem()] * 4,
        out_specs=(whole_vmem(),) * len(served),
        compiler_params=pltpu.CompilerParams(vmem_limit_bytes=6 * 2**20),
        name="pack",
    )(ancestors, own, other, noise, bias)


def across(left, right):
    return lax.dot_general(
        left, right, (((1,), (1,)), ((), ())), preferred_element_type=jnp.float32
    )


def identity(size):
    down = lax.broadcasted_iota(jnp.int32, (size, size), 0)
    along = lax.broadcasted_iota(jnp.int32, (size, size), 1)
    return jnp.where(down == along, 1.0, 0.0).astype(jnp.bfloat16)


def block_rows(position, rows):
    return pl.ds(pl.multiple_of(block_source(position) * rows, rows), rows)


def project(stream, w_ref, q_ref, k_ref, vt_ref, n_ref, eye, scale, rows):
    tokens, width = stream.shape
    normed = layer_norm(stream).astype(jnp.bfloat16)
    n_ref[...] = (
        jnp.dot(normed, w_ref[:, :width], preferred_element_type=jnp.float32) * scale
    ).astype(jnp.bfloat16)
    k_ref[...] = jnp.dot(
        normed, w_ref[:, width : 2 * width], preferred_element_type=jnp.float32
    ).astype(jnp.bfloat16)
    values = jnp.dot(
        normed, w_ref[:, 2 * width :], preferred_element_type=jnp.float32
    ).astype(jnp.bfloat16)
    for t in range(0, width, LANES):
        vt_ref[t : t + LANES, :] = across(eye, values[:, t : t + LANES]).astype(jnp.bfloat16)
    for p in range(tokens // rows):
        q_ref[p * rows : (p + 1) * rows, :] = n_ref[block_rows(p, rows), :]


def attend(groups, layer, ahead, rows, head_width, q_ref, k_ref, vt_ref, at_ref, work, eye, floor):
    s_buf, e_buf, n_buf = work
    half = q_ref.shape[1] // head_width // 2
    every = [(g * half + h, h, *group) for g, group in enumerate(groups) for h in range(half)]
    for slot, h, base, blocks in every:
        low = h * head_width
        high = low + head_width
        start = low // LANES * LANES
        stop = -(-high // LANES) * LANES
        lane = lax.broadcasted_iota(jnp.int32, (1, stop - start), 1) + start
        inside = jnp.where((lane >= low) & (lane < high), 1.0, 0.0).astype(jnp.bfloat16)
        cols = pl.ds(pl.multiple_of(base + start, LANES), stop - start)
        firsts = [(layer * half + h) * rows + (0 if p == 0 else ahead) for p in range(len(blocks))]
        bias = jnp.concatenate(
            [block[at : at + rows, :] for at, block in zip(firsts, blocks)], axis=0
        )
        s_buf[slot] = across(
            jnp.concatenate([k_ref[:, cols], eye], axis=1),
            jnp.concatenate([q_ref[:, cols] * inside, bias], axis=1),
        )
    for slot, h, base, blocks in every:
        scores = s_buf[slot] + floor
        raised = jnp.exp(scores - jnp.max(scores, axis=0, keepdims=True))
        n_buf[slot : slot + 1, :] = 1.0 / jnp.sum(raised, axis=0, keepdims=True)
        e_buf[slot] = raised.astype(jnp.bfloat16)
    for slot, h, base, blocks in every:
        own = pl.ds(pl.multiple_of(base + h * head_width, 16), head_width)
        out = jnp.dot(vt_ref[own, :], e_buf[slot], preferred_element_type=jnp.float32)
        at_ref[own, :] = (out * n_buf[slot : slot + 1, :]).astype(jnp.bfloat16)


def row_floor(mask_ref):
    anyone = jnp.max(mask_ref[...], axis=-1, keepdims=True)
    return jnp.where(anyone > 0, 0.0, MASKED).astype(jnp.float32)


def work_space(slots, tokens):
    return [
        pltpu.VMEM((slots, tokens, tokens), jnp.float32),
        pltpu.VMEM((slots, tokens, tokens), jnp.bfloat16),
        pltpu.VMEM((slots, tokens), jnp.float32),
    ]


def first_half(mask, kept, near, blocks, w_qkv, rows, heads, scale):
    sources = 1 + len(blocks)
    width = w_qkv.shape[1]
    tokens = sources * rows
    used = rows * (width // LANES)
    total = near.shape[0]

    def kernel(mask_ref, w_ref, kept_ref, near_ref, *refs):
        block_refs, refs = refs[: len(blocks)], refs[len(blocks) :]
        x_ref, q_ref, k_ref, vt_ref, at_ref, n_ref, *work = refs
        for p, block in enumerate((kept_ref, *block_refs)):
            at = used + total if p % 2 == 1 and p > 1 else 0
            for k in range(width // LANES):
                x_ref[block_rows(p, rows), k * LANES : (k + 1) * LANES] = block[
                    at + k * rows : at + (k + 1) * rows, :
                ]
        eye = identity(tokens)
        project(x_ref[...], w_ref.at[0], q_ref, k_ref, vt_ref, n_ref, eye, scale, rows)
        here = lax.axis_index("dom") * (width // 2)
        attend(
            [(here, (near_ref, *block_refs))], 0, used, rows, width // heads,
            q_ref, k_ref, vt_ref, at_ref, work, eye, row_floor(mask_ref),
        )

    wide = jax.ShapeDtypeStruct((tokens, width), jnp.bfloat16)
    tall = jax.ShapeDtypeStruct((width, tokens), jnp.bfloat16)
    return pl.pallas_call(
        kernel,
        out_shape=(wide, wide, wide, tall, tall),
        in_specs=[whole_vmem()] * (4 + len(blocks)),
        out_specs=(whole_vmem(),) * 5,
        scratch_shapes=[pltpu.VMEM((tokens, width), jnp.bfloat16)] + work_space(heads // 2, tokens),
        compiler_params=pltpu.CompilerParams(vmem_limit_bytes=8 * 2**20),
        cost_estimate=pl.CostEstimate(
            flops=6 * tokens * width * width, transcendentals=heads * tokens * tokens // 2,
            bytes_accessed=8 * width * width,
        ),
        name="first_half",
    )(mask, w_qkv, kept, near, *blocks)


def layers(mask, state, near, far, w_qkv, w_out, rows, heads, scale):
    sources = len(near)
    layer_count, width, _ = w_qkv.shape
    tokens = sources * rows
    used = rows * (width // LANES)

    def kernel(mask_ref, wq_ref, wo_ref, x_ref, q_in, k_in, vt_in, at_in, *refs):
        near_refs, far_refs, refs = refs[:sources], refs[sources : 2 * sources], refs[2 * sources :]
        out_ref, x_buf, q_buf, k_buf, vt_buf, at_buf, n_buf, *work = refs
        dom = lax.axis_index("dom")
        here = dom * (width // 2)
        there = (1 - dom) * (width // 2)
        floor = row_floor(mask_ref)
        eye = identity(tokens)
        ready = pl.ds(pl.multiple_of(here, LANES), width // 2)
        at_buf[ready, :] = at_in[ready, :]
        for l in range(layer_count):
            q_ref, k_ref, vt_ref = (q_in, k_in, vt_in) if l == 0 else (q_buf, k_buf, vt_buf)
            groups = [(there, far_refs)] if l == 0 else [(here, near_refs), (there, far_refs)]
            attend(
                groups, l, used, rows, width // heads, q_ref, k_ref, vt_ref, at_buf, work, eye, floor
            )
            together = across(eye, at_buf[...]).astype(jnp.bfloat16)
            for p in range(sources):
                n_buf[block_rows(p, rows), :] = together[p * rows : (p + 1) * rows, :]
            update = jnp.dot(n_buf[...], wo_ref[l], preferred_element_type=jnp.float32)
            before = x_ref[...] if l == 0 else x_buf[...]
            moved = (before.astype(jnp.float32) + update).astype(jnp.bfloat16)
            if l + 1 < layer_count:
                x_buf[...] = moved
                project(
                    moved, wq_ref.at[l + 1], q_buf, k_buf, vt_buf, n_buf, eye, scale, rows
                )
            else:
                for s in range(sources):
                    out_ref[s] = moved[s * rows : (s + 1) * rows, :]

    wide = pltpu.VMEM((tokens, width), jnp.bfloat16)
    tall = pltpu.VMEM((width, tokens), jnp.bfloat16)
    return pl.pallas_call(
        kernel,
        out_shape=jax.ShapeDtypeStruct((sources, rows, width), jnp.bfloat16),
        in_specs=[whole_vmem()] * (8 + 2 * sources),
        out_specs=whole_vmem(),
        scratch_shapes=[wide, wide, wide, tall, tall, wide] + work_space(heads, tokens),
        compiler_params=pltpu.CompilerParams(vmem_limit_bytes=8 * 2**20),
        cost_estimate=pl.CostEstimate(
            flops=14 * tokens * width * width, transcendentals=2 * heads * tokens * tokens,
            bytes_accessed=10 * width * width,
        ),
        name="layers",
    )(mask, w_qkv, w_out, *state, *near, *far)


def spread_body(states, ancestors, noise, pair, token_mask, w_qkv, w_out, w_pair):
    particles, rows, width = states.shape
    heads = w_pair.shape[2]
    scale = (width // heads) ** (-0.5)
    swap = [(0, 1), (1, 0)]
    mask_row = token_mask.reshape(1, -1)

    def beside(block, k=1):
        return lax.ppermute(block, "tok", [(t, t ^ k) for t in range(particles)])

    other_states = lax.ppermute(states, "dom", swap)
    near, far, own, local_noise = prepare(
        pair, mask_row, w_pair.transpose(0, 2, 1), states, noise, w_qkv
    )
    kept, neighbour, *sent = pack(ancestors, own, other_states, local_noise, near)
    blocks = {}
    for k in range(particles - 2, 0, -2):
        blocks[k] = beside(sent[k // 2 - 1], k)
        blocks[k + 1] = beside(blocks[k])
    blocks[1] = beside(neighbour)
    blocks = [blocks[p] for p in range(1, particles)]
    swapped = [lax.ppermute(block, "dom", swap) for block in blocks]
    state = first_half(mask_row, kept, near, blocks, w_qkv, rows, heads, scale)
    result = layers(
        mask_row, state, (near, *blocks), (far, *swapped), w_qkv, w_out, rows, heads, scale
    )
    return lax.all_to_all(result, "tok", 0, 0, tiled=True)


def solution(mesh):
    placed = (
        P(("groups", "dom"), "tok", None),
        P(("groups", "dom")),
        P(("groups", "dom"), "tok", None),
        P(("groups", "tok"), None, None),
        P("groups"),
        P(),
        P(),
        P(),
    )

    def body(states, ancestors, noise, pair, token_mask, w_qkv, w_out, w_pair):
        particles, rows, width = states.shape
        fits = (
            particles == mesh.shape["tok"]
            and particles & (particles - 1) == 0
            and particles > 2
            and mesh.shape["dom"] == 2
            and width % (2 * LANES) == 0
            and w_pair.shape[2] % 2 == 0
            and pair.shape[1] == LANES
            and pair.shape[2] == LANES
            and rows % 16 == 0
            and (width // w_pair.shape[2]) % 16 == 0
        )
        chosen = spread_body if fits else gathered_body
        return chosen(states, ancestors, noise, pair, token_mask, w_qkv, w_out, w_pair)

    return jax.shard_map(
        body,
        mesh=mesh,
        in_specs=placed,
        out_specs=P(("groups", "dom"), "tok", None),
        check_vma=False,
    )
```

```python
import jax
import jax.numpy as jnp
from jax import lax
from jax.experimental import pallas as pl
from jax.experimental.pallas import tpu as pltpu
from jax.sharding import PartitionSpec as P

MASKED = -1000000000.0
LANES = 128


def layer_norm(stream):
    values = stream.astype(jnp.float32)
    average = jnp.mean(values, axis=-1, keepdims=True)
    centred = values - average
    spread = jnp.mean(centred * centred, axis=-1, keepdims=True)
    return centred * lax.rsqrt(spread + 1e-05)


def gathered_body(states, ancestors, noise, pair, token_mask, w_qkv, w_out, w_pair):
    part_count = states.shape[0]
    tok_rows = states.shape[1]
    model_width = states.shape[2]
    head_count = w_pair.shape[2]
    head_width = model_width // head_count
    layer_count = w_qkv.shape[0]
    total_keys = pair.shape[1]
    everyone = lax.all_gather(states, "dom", axis=0, tiled=True)
    chosen = jnp.take(everyone, ancestors, axis=0)
    stream = (chosen.astype(jnp.float32) + 0.5 * noise.astype(jnp.float32)).astype(jnp.bfloat16)
    penalty = jnp.where(token_mask > 0, 0.0, MASKED).astype(jnp.float32)
    pair_terms = jnp.einsum("ijc,lch->lhij", pair, w_pair, preferred_element_type=jnp.float32)
    full_bias = pair_terms + penalty[None, None, None, :]
    query_scale = head_width ** (-0.5)
    for layer_index in range(layer_count):
        normed = layer_norm(stream).astype(jnp.bfloat16)
        projected = jnp.dot(
            normed.reshape(part_count * tok_rows, model_width),
            w_qkv[layer_index],
            preferred_element_type=jnp.float32,
        )
        projected = projected.reshape(part_count, tok_rows, 3 * model_width)
        query = (projected[..., :model_width] * query_scale).astype(jnp.bfloat16)
        both = projected[..., model_width:].astype(jnp.bfloat16)
        query_heads = query.reshape(part_count, tok_rows, head_count, head_width)
        gathered = lax.all_gather(both, "tok", axis=1, tiled=True)
        all_keys, all_values = gathered[..., :model_width], gathered[..., model_width:]
        key_heads = all_keys.reshape(part_count, total_keys, head_count, head_width)
        scores = (
            jnp.einsum(
                "pihe,pjhe->phij", query_heads, key_heads, preferred_element_type=jnp.float32
            )
            + full_bias[layer_index][None]
        )
        weights = jax.nn.softmax(scores, axis=-1).astype(jnp.bfloat16)
        value_heads = all_values.reshape(part_count, total_keys, head_count, head_width)
        attended = jnp.einsum(
            "phij,pjhe->pihe", weights, value_heads, preferred_element_type=jnp.float32
        ).astype(jnp.bfloat16)
        attended = attended.reshape(part_count * tok_rows, model_width)
        update = jnp.dot(attended, w_out[layer_index], preferred_element_type=jnp.float32)
        update = update.reshape(part_count, tok_rows, model_width)
        stream = (stream.astype(jnp.float32) + update).astype(jnp.bfloat16)
    return stream


def whole_vmem():
    return pl.BlockSpec(memory_space=pltpu.VMEM)


def in_hbm():
    return pl.BlockSpec(memory_space=pltpu.HBM)


def stay(array):
    return pltpu.with_memory_space_constraint(array, pltpu.HBM)


def in_smem():
    return pl.BlockSpec(memory_space=pltpu.SMEM)


def prepare(pair, mask_row, w_rows, own, noise, w_qkv):
    rows, keys, channels = pair.shape
    layer_count, heads, _ = w_rows.shape
    half = heads // 2
    blocks = layer_count * heads

    def kernel(
        pair_hbm, mask_hbm, w_hbm, own_hbm, noise_hbm, wq_hbm,
        near_ref, far_ref, own_ref, noise_ref, pair_ref, mask_ref, w_ref, rows_ref, sem,
    ):
        copies = [
            pltpu.make_async_copy(mask_hbm, mask_ref, sem.at[0]),
            pltpu.make_async_copy(w_hbm, w_ref, sem.at[1]),
            pltpu.make_async_copy(pair_hbm, pair_ref, sem.at[2]),
            pltpu.make_async_copy(own_hbm, own_ref, sem.at[3]),
            pltpu.make_async_copy(noise_hbm, noise_ref, sem.at[4]),
        ]
        for copy in copies:
            copy.start()
        copies[0].wait()
        copies[1].wait()
        penalty = jnp.where(mask_ref[...] > 0, 0.0, MASKED).astype(jnp.float32)
        w_all = w_ref[...].reshape(blocks, channels)
        copies[2].wait()
        for i in range(rows):
            piece = across(w_all, pair_ref[i]) + penalty
            rows_ref[:, i, :] = piece - jnp.max(piece, axis=-1, keepdims=True)
        dom = lax.axis_index("dom")
        for l in range(layer_count):
            for h in range(half):
                at = (l * half + h) * rows
                near = l * heads + dom * half + h
                far = l * heads + (1 - dom) * half + h
                near_ref[at : at + rows, :] = rows_ref[near].astype(jnp.bfloat16)
                far_ref[at : at + rows, :] = rows_ref[far].astype(jnp.bfloat16)
        for copy in copies[3:]:
            copy.wait()

    part = jax.ShapeDtypeStruct((blocks // 2 * rows, keys), jnp.bfloat16)
    return pl.pallas_call(
        kernel,
        out_shape=(
            part, part,
            jax.ShapeDtypeStruct(own.shape, own.dtype),
            jax.ShapeDtypeStruct(noise.shape, noise.dtype),
        ),
        in_specs=[in_hbm()] * 6,
        out_specs=(whole_vmem(),) * 4,
        scratch_shapes=[
            pltpu.VMEM(pair.shape, pair.dtype),
            pltpu.VMEM(mask_row.shape, mask_row.dtype),
            pltpu.VMEM(w_rows.shape, w_rows.dtype),
            pltpu.VMEM((blocks, rows, keys), jnp.float32),
            pltpu.SemaphoreType.DMA((5,)),
        ],
        cost_estimate=pl.CostEstimate(
            flops=2 * blocks * rows * keys * channels, transcendentals=0, bytes_accessed=8000000
        ),
        compiler_params=pltpu.CompilerParams(vmem_limit_bytes=6 * 2**20),
        name="prepare",
    )(*(stay(a) for a in (pair, mask_row, w_rows, own, noise, w_qkv)))


def block_source(position):
    return jnp.bitwise_xor(lax.axis_index("tok"), position)


def pack(ancestors, own, other, noise, bias):
    particles, rows, width = own.shape
    used = rows * (width // LANES)
    total = bias.shape[0]
    served = [0, 1] + list(range(2, particles, 2))

    def kernel(anc_ref, own_ref, other_ref, noise_ref, bias_ref, *outs):
        dom = lax.axis_index("dom")

        def put(out_ref, first, particle):
            ancestor = anc_ref[particle]
            local = lax.rem(ancestor, particles)
            mine = lax.div(ancestor, particles) == dom
            value = jnp.where(mine, own_ref[local], other_ref[local])
            value = value.astype(jnp.float32) + 0.5 * noise_ref[particle].astype(jnp.float32)
            value = value.astype(jnp.bfloat16)
            for k in range(width // LANES):
                out_ref[first + k * rows : first + (k + 1) * rows, :] = value[
                    :, k * LANES : (k + 1) * LANES
                ]

        for position, out_ref in zip(served, outs):
            put(out_ref, 0, block_source(position))
            if position > 0:
                out_ref[used : used + total, :] = bias_ref[...]
            if position > 1:
                put(out_ref, used + total, block_source(position + 1))

    lengths = [used, used + total] + [total + 2 * used] * (len(served) - 2)
    return pl.pallas_call(
        kernel,
        out_shape=tuple(jax.ShapeDtypeStruct((length, LANES), own.dtype) for length in lengths),
        in_specs=[in_smem()] + [whole_vmem()] * 4,
        out_specs=(whole_vmem(),) * len(served),
        compiler_params=pltpu.CompilerParams(vmem_limit_bytes=6 * 2**20),
        name="pack",
    )(ancestors, own, other, noise, bias)


def across(left, right):
    return lax.dot_general(
        left, right, (((1,), (1,)), ((), ())), preferred_element_type=jnp.float32
    )


def identity(size):
    down = lax.broadcasted_iota(jnp.int32, (size, size), 0)
    along = lax.broadcasted_iota(jnp.int32, (size, size), 1)
    return jnp.where(down == along, 1.0, 0.0).astype(jnp.bfloat16)


def block_rows(position, rows):
    return pl.ds(pl.multiple_of(block_source(position) * rows, rows), rows)


def project(stream, w_ref, q_ref, k_ref, vt_ref, n_ref, eye, scale, rows):
    tokens, width = stream.shape
    normed = layer_norm(stream).astype(jnp.bfloat16)
    n_ref[...] = (
        jnp.dot(normed, w_ref[:, :width], preferred_element_type=jnp.float32) * scale
    ).astype(jnp.bfloat16)
    k_ref[...] = jnp.dot(
        normed, w_ref[:, width : 2 * width], preferred_element_type=jnp.float32
    ).astype(jnp.bfloat16)
    values = jnp.dot(
        normed, w_ref[:, 2 * width :], preferred_element_type=jnp.float32
    ).astype(jnp.bfloat16)
    for t in range(0, width, LANES):
        vt_ref[t : t + LANES, :] = across(eye, values[:, t : t + LANES]).astype(jnp.bfloat16)
    for p in range(tokens // rows):
        q_ref[p * rows : (p + 1) * rows, :] = n_ref[block_rows(p, rows), :]


def attend(groups, layer, ahead, rows, head_width, q_ref, k_ref, vt_ref, at_ref, work, eye, floor):
    s_buf, e_buf, n_buf = work
    half = q_ref.shape[1] // head_width // 2
    every = [(g * half + h, h, *group) for g, group in enumerate(groups) for h in range(half)]
    for slot, h, base, blocks in every:
        low = h * head_width
        high = low + head_width
        start = low // LANES * LANES
        stop = -(-high // LANES) * LANES
        lane = lax.broadcasted_iota(jnp.int32, (1, stop - start), 1) + start
        inside = jnp.where((lane >= low) & (lane < high), 1.0, 0.0).astype(jnp.bfloat16)
        cols = pl.ds(pl.multiple_of(base + start, LANES), stop - start)
        firsts = [(layer * half + h) * rows + (0 if p == 0 or p % 2 == 1 and p > 1 else ahead) for p in range(len(blocks))]
        bias = jnp.concatenate(
            [block[at : at + rows, :] for at, block in zip(firsts, blocks)], axis=0
        )
        s_buf[slot] = across(
            jnp.concatenate([k_ref[:, cols], eye], axis=1),
            jnp.concatenate([q_ref[:, cols] * inside, bias], axis=1),
        )
    for slot, h, base, blocks in every:
        scores = s_buf[slot] + floor
        raised = jnp.exp(scores - jnp.max(scores, axis=0, keepdims=True))
        n_buf[slot : slot + 1, :] = 1.0 / jnp.sum(raised, axis=0, keepdims=True)
        e_buf[slot] = raised.astype(jnp.bfloat16)
    for slot, h, base, blocks in every:
        own = pl.ds(pl.multiple_of(base + h * head_width, 16), head_width)
        out = jnp.dot(vt_ref[own, :], e_buf[slot], preferred_element_type=jnp.float32)
        at_ref[own, :] = (out * n_buf[slot : slot + 1, :]).astype(jnp.bfloat16)


def row_floor(mask_ref):
    anyone = jnp.max(mask_ref[...], axis=-1, keepdims=True)
    return jnp.where(anyone > 0, 0.0, MASKED).astype(jnp.float32)


def work_space(slots, tokens):
    return [
        pltpu.VMEM((slots, tokens, tokens), jnp.float32),
        pltpu.VMEM((slots, tokens, tokens), jnp.bfloat16),
        pltpu.VMEM((slots, tokens), jnp.float32),
    ]


def first_half(mask, kept, near, blocks, w_qkv, rows, heads, scale):
    sources = 1 + len(blocks)
    width = w_qkv.shape[1]
    tokens = sources * rows
    used = rows * (width // LANES)
    total = near.shape[0]

    def kernel(mask_ref, w_ref, kept_ref, near_ref, *refs):
        block_refs, refs = refs[: len(blocks)], refs[len(blocks) :]
        x_ref, q_ref, k_ref, vt_ref, at_ref, n_ref, *work = refs
        for p, block in enumerate((kept_ref, *block_refs)):
            at = total if p % 2 == 1 and p > 1 else 0
            for k in range(width // LANES):
                x_ref[block_rows(p, rows), k * LANES : (k + 1) * LANES] = block[
                    at + k * rows : at + (k + 1) * rows, :
                ]
        eye = identity(tokens)
        project(x_ref[...], w_ref.at[0], q_ref, k_ref, vt_ref, n_ref, eye, scale, rows)
        here = lax.axis_index("dom") * (width // 2)
        attend(
            [(here, (near_ref, *block_refs))], 0, used, rows, width // heads,
            q_ref, k_ref, vt_ref, at_ref, work, eye, row_floor(mask_ref),
        )

    wide = jax.ShapeDtypeStruct((tokens, width), jnp.bfloat16)
    tall = jax.ShapeDtypeStruct((width, tokens), jnp.bfloat16)
    return pl.pallas_call(
        kernel,
        out_shape=(wide, wide, wide, tall, tall),
        in_specs=[whole_vmem()] * (4 + len(blocks)),
        out_specs=(whole_vmem(),) * 5,
        scratch_shapes=[pltpu.VMEM((tokens, width), jnp.bfloat16)] + work_space(heads // 2, tokens),
        compiler_params=pltpu.CompilerParams(vmem_limit_bytes=8 * 2**20),
        cost_estimate=pl.CostEstimate(
            flops=6 * tokens * width * width, transcendentals=heads * tokens * tokens // 2,
            bytes_accessed=8 * width * width,
        ),
        name="first_half",
    )(mask, w_qkv, kept, near, *blocks)


def layers(mask, state, near, far, w_qkv, w_out, rows, heads, scale):
    sources = len(near)
    layer_count, width, _ = w_qkv.shape
    tokens = sources * rows
    used = rows * (width // LANES)

    def kernel(mask_ref, wq_ref, wo_ref, x_ref, q_in, k_in, vt_in, at_in, *refs):
        near_refs, far_refs, refs = refs[:sources], refs[sources : 2 * sources], refs[2 * sources :]
        out_ref, x_buf, q_buf, k_buf, vt_buf, at_buf, n_buf, *work = refs
        dom = lax.axis_index("dom")
        here = dom * (width // 2)
        there = (1 - dom) * (width // 2)
        floor = row_floor(mask_ref)
        eye = identity(tokens)
        ready = pl.ds(pl.multiple_of(here, LANES), width // 2)
        at_buf[ready, :] = at_in[ready, :]
        for l in range(layer_count):
            q_ref, k_ref, vt_ref = (q_in, k_in, vt_in) if l == 0 else (q_buf, k_buf, vt_buf)
            groups = [(there, far_refs)] if l == 0 else [(here, near_refs), (there, far_refs)]
            attend(
                groups, l, used, rows, width // heads, q_ref, k_ref, vt_ref, at_buf, work, eye, floor
            )
            together = across(eye, at_buf[...]).astype(jnp.bfloat16)
            for p in range(sources):
                n_buf[block_rows(p, rows), :] = together[p * rows : (p + 1) * rows, :]
            update = jnp.dot(n_buf[...], wo_ref[l], preferred_element_type=jnp.float32)
            before = x_ref[...] if l == 0 else x_buf[...]
            moved = (before.astype(jnp.float32) + update).astype(jnp.bfloat16)
            if l + 1 < layer_count:
                x_buf[...] = moved
                project(
                    moved, wq_ref.at[l + 1], q_buf, k_buf, vt_buf, n_buf, eye, scale, rows
                )
            else:
                for s in range(sources):
                    out_ref[s] = moved[s * rows : (s + 1) * rows, :]

    wide = pltpu.VMEM((tokens, width), jnp.bfloat16)
    tall = pltpu.VMEM((width, tokens), jnp.bfloat16)
    return pl.pallas_call(
        kernel,
        out_shape=jax.ShapeDtypeStruct((sources, rows, width), jnp.bfloat16),
        in_specs=[whole_vmem()] * (8 + 2 * sources),
        out_specs=whole_vmem(),
        scratch_shapes=[wide, wide, wide, tall, tall, wide] + work_space(heads, tokens),
        compiler_params=pltpu.CompilerParams(vmem_limit_bytes=8 * 2**20),
        cost_estimate=pl.CostEstimate(
            flops=14 * tokens * width * width, transcendentals=2 * heads * tokens * tokens,
            bytes_accessed=10 * width * width,
        ),
        name="layers",
    )(mask, w_qkv, w_out, *state, *near, *far)


def apart(joined, parts):
    pieces, at = [], 0
    for part in parts:
        pieces.append(joined[at : at + part.shape[0]])
        at += part.shape[0]
    return pieces


def spread_body(states, ancestors, noise, pair, token_mask, w_qkv, w_out, w_pair):
    particles, rows, width = states.shape
    heads = w_pair.shape[2]
    scale = (width // heads) ** (-0.5)
    swap = [(0, 1), (1, 0)]
    mask_row = token_mask.reshape(1, -1)

    def beside(block, k=1):
        return lax.ppermute(block, "tok", [(t, t ^ k) for t in range(particles)])

    other_states = lax.ppermute(states, "dom", swap)
    near, rest, own, local_noise = prepare(
        pair, mask_row, w_pair.transpose(0, 2, 1), states, noise, w_qkv
    )
    kept, neighbour, *sent = pack(ancestors, own, other_states, local_noise, near)
    ahead = rows * (width // LANES)
    passing = range(2, particles, 2)
    blocks = {k: beside(block, k) for k, block in zip(passing, sent)}
    blocks[1], blocks[3] = apart(
        beside(jnp.concatenate([neighbour, blocks[2][ahead:]], axis=0)), [neighbour, blocks[2][ahead:]]
    )
    for k in passing[1:-1]:
        blocks[k + 1] = beside(blocks[k][ahead:])
    far = {}

    def swap_all(distances):
        group = [blocks[distance] for distance in distances]
        swapped = lax.ppermute(jnp.concatenate(group, axis=0), "dom", swap)
        far.update(zip(distances, apart(swapped, group)))

    blocks[passing[-1] + 1] = beside(blocks[passing[-1]][ahead:])
    for k in passing:
        swap_all([k])
    swap_all(list(range(1, particles - 1, 2)))
    swap_all([particles - 1])
    swapped = [far[distance] for distance in range(1, particles)]
    blocks = [blocks[distance] for distance in range(1, particles)]
    state = first_half(mask_row, kept, near, blocks, w_qkv, rows, heads, scale)
    result = layers(
        mask_row, state, (near, *blocks), (rest, *swapped), w_qkv, w_out, rows, heads, scale
    )
    return lax.all_to_all(result, "tok", 0, 0, tiled=True)


def solution(mesh):
    placed = (
        P(("groups", "dom"), "tok", None),
        P(("groups", "dom")),
        P(("groups", "dom"), "tok", None),
        P(("groups", "tok"), None, None),
        P("groups"),
        P(),
        P(),
        P(),
    )

    def body(states, ancestors, noise, pair, token_mask, w_qkv, w_out, w_pair):
        particles, rows, width = states.shape
        fits = (
            particles == mesh.shape["tok"]
            and particles & (particles - 1) == 0
            and particles > 4
            and mesh.shape["dom"] == 2
            and width % (2 * LANES) == 0
            and w_pair.shape[2] % 2 == 0
            and pair.shape[1] == LANES
            and pair.shape[2] == LANES
            and rows % 16 == 0
            and (width // w_pair.shape[2]) % 16 == 0
        )
        chosen = spread_body if fits else gathered_body
        return chosen(states, ancestors, noise, pair, token_mask, w_qkv, w_out, w_pair)

    return jax.shard_map(
        body,
        mesh=mesh,
        in_specs=placed,
        out_specs=P(("groups", "dom"), "tok", None),
        check_vma=False,
    )
```

```python
import jax
import jax.numpy as jnp
from jax import lax
from jax.experimental import pallas as pl
from jax.experimental.pallas import tpu as pltpu
from jax.sharding import PartitionSpec as P

MASKED = -1000000000.0
LANES = 128


def layer_norm(stream):
    values = stream.astype(jnp.float32)
    average = jnp.mean(values, axis=-1, keepdims=True)
    centred = values - average
    spread = jnp.mean(centred * centred, axis=-1, keepdims=True)
    return centred * lax.rsqrt(spread + 1e-05)


def gathered_body(states, ancestors, noise, pair, token_mask, w_qkv, w_out, w_pair):
    part_count = states.shape[0]
    tok_rows = states.shape[1]
    model_width = states.shape[2]
    head_count = w_pair.shape[2]
    head_width = model_width // head_count
    layer_count = w_qkv.shape[0]
    total_keys = pair.shape[1]
    everyone = lax.all_gather(states, "dom", axis=0, tiled=True)
    chosen = jnp.take(everyone, ancestors, axis=0)
    stream = (chosen.astype(jnp.float32) + 0.5 * noise.astype(jnp.float32)).astype(jnp.bfloat16)
    penalty = jnp.where(token_mask > 0, 0.0, MASKED).astype(jnp.float32)
    pair_terms = jnp.einsum("ijc,lch->lhij", pair, w_pair, preferred_element_type=jnp.float32)
    full_bias = pair_terms + penalty[None, None, None, :]
    query_scale = head_width ** (-0.5)
    for layer_index in range(layer_count):
        normed = layer_norm(stream).astype(jnp.bfloat16)
        projected = jnp.dot(
            normed.reshape(part_count * tok_rows, model_width),
            w_qkv[layer_index],
            preferred_element_type=jnp.float32,
        )
        projected = projected.reshape(part_count, tok_rows, 3 * model_width)
        query = (projected[..., :model_width] * query_scale).astype(jnp.bfloat16)
        both = projected[..., model_width:].astype(jnp.bfloat16)
        query_heads = query.reshape(part_count, tok_rows, head_count, head_width)
        gathered = lax.all_gather(both, "tok", axis=1, tiled=True)
        all_keys, all_values = gathered[..., :model_width], gathered[..., model_width:]
        key_heads = all_keys.reshape(part_count, total_keys, head_count, head_width)
        scores = (
            jnp.einsum(
                "pihe,pjhe->phij", query_heads, key_heads, preferred_element_type=jnp.float32
            )
            + full_bias[layer_index][None]
        )
        weights = jax.nn.softmax(scores, axis=-1).astype(jnp.bfloat16)
        value_heads = all_values.reshape(part_count, total_keys, head_count, head_width)
        attended = jnp.einsum(
            "phij,pjhe->pihe", weights, value_heads, preferred_element_type=jnp.float32
        ).astype(jnp.bfloat16)
        attended = attended.reshape(part_count * tok_rows, model_width)
        update = jnp.dot(attended, w_out[layer_index], preferred_element_type=jnp.float32)
        update = update.reshape(part_count, tok_rows, model_width)
        stream = (stream.astype(jnp.float32) + update).astype(jnp.bfloat16)
    return stream


def whole_vmem():
    return pl.BlockSpec(memory_space=pltpu.VMEM)


def in_hbm():
    return pl.BlockSpec(memory_space=pltpu.HBM)


def stay(array):
    return pltpu.with_memory_space_constraint(array, pltpu.HBM)


def in_smem():
    return pl.BlockSpec(memory_space=pltpu.SMEM)


def prepare(pair, mask_row, w_rows, own, noise, w_qkv):
    rows, keys, channels = pair.shape
    layer_count, heads, _ = w_rows.shape
    half = heads // 2
    blocks = layer_count * heads

    def kernel(
        pair_hbm, mask_hbm, w_hbm, own_hbm, noise_hbm, wq_hbm,
        near_ref, far_ref, own_ref, noise_ref, pair_ref, mask_ref, w_ref, rows_ref, sem,
    ):
        copies = [
            pltpu.make_async_copy(mask_hbm, mask_ref, sem.at[0]),
            pltpu.make_async_copy(w_hbm, w_ref, sem.at[1]),
            pltpu.make_async_copy(pair_hbm, pair_ref, sem.at[2]),
            pltpu.make_async_copy(own_hbm, own_ref, sem.at[3]),
            pltpu.make_async_copy(noise_hbm, noise_ref, sem.at[4]),
        ]
        for copy in copies:
            copy.start()
        copies[0].wait()
        copies[1].wait()
        penalty = jnp.where(mask_ref[...] > 0, 0.0, MASKED).astype(jnp.float32)
        w_all = w_ref[...].reshape(blocks, channels)
        copies[2].wait()
        terms = across(w_all, pair_ref[...].reshape(rows * keys, channels))
        for i in range(rows):
            piece = terms[:, i * keys : (i + 1) * keys] + penalty
            rows_ref[:, i, :] = piece - jnp.max(piece, axis=-1, keepdims=True)
        dom = lax.axis_index("dom")
        for l in range(layer_count):
            for h in range(half):
                at = (l * half + h) * rows
                near = l * heads + dom * half + h
                far = l * heads + (1 - dom) * half + h
                near_ref[at : at + rows, :] = rows_ref[near].astype(jnp.bfloat16)
                far_ref[at : at + rows, :] = rows_ref[far].astype(jnp.bfloat16)
        for copy in copies[3:]:
            copy.wait()

    part = jax.ShapeDtypeStruct((blocks // 2 * rows, keys), jnp.bfloat16)
    return pl.pallas_call(
        kernel,
        out_shape=(
            part, part,
            jax.ShapeDtypeStruct(own.shape, own.dtype),
            jax.ShapeDtypeStruct(noise.shape, noise.dtype),
        ),
        in_specs=[in_hbm()] * 6,
        out_specs=(whole_vmem(),) * 4,
        scratch_shapes=[
            pltpu.VMEM(pair.shape, pair.dtype),
            pltpu.VMEM(mask_row.shape, mask_row.dtype),
            pltpu.VMEM(w_rows.shape, w_rows.dtype),
            pltpu.VMEM((blocks, rows, keys), jnp.float32),
            pltpu.SemaphoreType.DMA((5,)),
        ],
        cost_estimate=pl.CostEstimate(
            flops=2 * blocks * rows * keys * channels, transcendentals=0, bytes_accessed=8000000
        ),
        compiler_params=pltpu.CompilerParams(vmem_limit_bytes=6 * 2**20),
        name="prepare",
    )(*(stay(a) for a in (pair, mask_row, w_rows, own, noise, w_qkv)))


def block_source(position):
    return jnp.bitwise_xor(lax.axis_index("tok"), position)


def pack(ancestors, own, other, noise, bias):
    particles, rows, width = own.shape
    used = rows * (width // LANES)
    total = bias.shape[0]
    served = [0, 1] + list(range(2, particles, 2))

    def kernel(anc_ref, own_ref, other_ref, noise_ref, bias_ref, *outs):
        dom = lax.axis_index("dom")

        def put(out_ref, first, particle):
            ancestor = anc_ref[particle]
            local = lax.rem(ancestor, particles)
            mine = lax.div(ancestor, particles) == dom
            value = jnp.where(mine, own_ref[local], other_ref[local])
            value = value.astype(jnp.float32) + 0.5 * noise_ref[particle].astype(jnp.float32)
            value = value.astype(jnp.bfloat16)
            for k in range(width // LANES):
                out_ref[first + k * rows : first + (k + 1) * rows, :] = value[
                    :, k * LANES : (k + 1) * LANES
                ]

        for position, out_ref in zip(served, outs):
            put(out_ref, 0, block_source(position))
            if position > 0:
                out_ref[used : used + total, :] = bias_ref[...]
            if position > 1:
                put(out_ref, used + total, block_source(position + 1))

    lengths = [used, used + total] + [total + 2 * used] * (len(served) - 2)
    return pl.pallas_call(
        kernel,
        out_shape=tuple(jax.ShapeDtypeStruct((length, LANES), own.dtype) for length in lengths),
        in_specs=[in_smem()] + [whole_vmem()] * 4,
        out_specs=(whole_vmem(),) * len(served),
        compiler_params=pltpu.CompilerParams(vmem_limit_bytes=6 * 2**20),
        name="pack",
    )(ancestors, own, other, noise, bias)


def across(left, right):
    return lax.dot_general(
        left, right, (((1,), (1,)), ((), ())), preferred_element_type=jnp.float32
    )


def identity(size):
    down = lax.broadcasted_iota(jnp.int32, (size, size), 0)
    along = lax.broadcasted_iota(jnp.int32, (size, size), 1)
    return jnp.where(down == along, 1.0, 0.0).astype(jnp.bfloat16)


def block_rows(position, rows):
    return pl.ds(pl.multiple_of(block_source(position) * rows, rows), rows)


def project(stream, w_ref, q_ref, k_ref, vt_ref, n_ref, eye, scale, rows):
    tokens, width = stream.shape
    normed = layer_norm(stream).astype(jnp.bfloat16)
    n_ref[...] = (
        jnp.dot(normed, w_ref[:, :width], preferred_element_type=jnp.float32) * scale
    ).astype(jnp.bfloat16)
    k_ref[...] = jnp.dot(
        normed, w_ref[:, width : 2 * width], preferred_element_type=jnp.float32
    ).astype(jnp.bfloat16)
    values = jnp.dot(
        normed, w_ref[:, 2 * width :], preferred_element_type=jnp.float32
    ).astype(jnp.bfloat16)
    for t in range(0, width, LANES):
        vt_ref[t : t + LANES, :] = across(eye, values[:, t : t + LANES]).astype(jnp.bfloat16)
    for p in range(tokens // rows):
        q_ref[p * rows : (p + 1) * rows, :] = n_ref[block_rows(p, rows), :]


def attend(groups, layer, ahead, rows, head_width, q_ref, k_ref, vt_ref, at_ref, work, eye, floor):
    s_buf, e_buf, n_buf = work
    half = q_ref.shape[1] // head_width // 2
    every = [(g * half + h, h, *group) for g, group in enumerate(groups) for h in range(half)]
    for slot, h, base, blocks in every:
        low = h * head_width
        high = low + head_width
        start = low // LANES * LANES
        stop = -(-high // LANES) * LANES
        lane = lax.broadcasted_iota(jnp.int32, (1, stop - start), 1) + start
        inside = jnp.where((lane >= low) & (lane < high), 1.0, 0.0).astype(jnp.bfloat16)
        cols = pl.ds(pl.multiple_of(base + start, LANES), stop - start)
        firsts = [(layer * half + h) * rows + (0 if p == 0 or p % 2 == 1 and p > 1 else ahead) for p in range(len(blocks))]
        bias = jnp.concatenate(
            [block[at : at + rows, :] for at, block in zip(firsts, blocks)], axis=0
        )
        s_buf[slot] = across(
            jnp.concatenate([k_ref[:, cols], eye], axis=1),
            jnp.concatenate([q_ref[:, cols] * inside, bias], axis=1),
        )
    for slot, h, base, blocks in every:
        scores = s_buf[slot] + floor
        raised = jnp.exp(scores - jnp.max(scores, axis=0, keepdims=True))
        n_buf[slot : slot + 1, :] = 1.0 / jnp.sum(raised, axis=0, keepdims=True)
        e_buf[slot] = raised.astype(jnp.bfloat16)
    for slot, h, base, blocks in every:
        own = pl.ds(pl.multiple_of(base + h * head_width, 16), head_width)
        out = jnp.dot(vt_ref[own, :], e_buf[slot], preferred_element_type=jnp.float32)
        at_ref[own, :] = (out * n_buf[slot : slot + 1, :]).astype(jnp.bfloat16)


def row_floor(mask_ref):
    anyone = jnp.max(mask_ref[...], axis=-1, keepdims=True)
    return jnp.where(anyone > 0, 0.0, MASKED).astype(jnp.float32)


def work_space(slots, tokens):
    return [
        pltpu.VMEM((slots, tokens, tokens), jnp.float32),
        pltpu.VMEM((slots, tokens, tokens), jnp.bfloat16),
        pltpu.VMEM((slots, tokens), jnp.float32),
    ]


def first_half(mask, kept, near, blocks, w_qkv, rows, heads, scale):
    sources = 1 + len(blocks)
    width = w_qkv.shape[1]
    tokens = sources * rows
    used = rows * (width // LANES)
    total = near.shape[0]

    def kernel(mask_ref, w_ref, kept_ref, near_ref, *refs):
        block_refs, refs = refs[: len(blocks)], refs[len(blocks) :]
        x_ref, q_ref, k_ref, vt_ref, at_ref, n_ref, *work = refs
        for p, block in enumerate((kept_ref, *block_refs)):
            at = total if p % 2 == 1 and p > 1 else 0
            for k in range(width // LANES):
                x_ref[block_rows(p, rows), k * LANES : (k + 1) * LANES] = block[
                    at + k * rows : at + (k + 1) * rows, :
                ]
        eye = identity(tokens)
        project(x_ref[...], w_ref.at[0], q_ref, k_ref, vt_ref, n_ref, eye, scale, rows)
        here = lax.axis_index("dom") * (width // 2)
        attend(
            [(here, (near_ref, *block_refs))], 0, used, rows, width // heads,
            q_ref, k_ref, vt_ref, at_ref, work, eye, row_floor(mask_ref),
        )

    wide = jax.ShapeDtypeStruct((tokens, width), jnp.bfloat16)
    tall = jax.ShapeDtypeStruct((width, tokens), jnp.bfloat16)
    return pl.pallas_call(
        kernel,
        out_shape=(wide, wide, wide, tall, tall),
        in_specs=[whole_vmem()] * (4 + len(blocks)),
        out_specs=(whole_vmem(),) * 5,
        scratch_shapes=[pltpu.VMEM((tokens, width), jnp.bfloat16)] + work_space(heads // 2, tokens),
        compiler_params=pltpu.CompilerParams(vmem_limit_bytes=8 * 2**20),
        cost_estimate=pl.CostEstimate(
            flops=6 * tokens * width * width, transcendentals=heads * tokens * tokens // 2,
            bytes_accessed=8 * width * width,
        ),
        name="first_half",
    )(mask, w_qkv, kept, near, *blocks)


def layers(mask, state, near, far, w_qkv, w_out, rows, heads, scale):
    sources = len(near)
    layer_count, width, _ = w_qkv.shape
    tokens = sources * rows
    used = rows * (width // LANES)

    def kernel(mask_ref, wq_ref, wo_ref, x_ref, q_in, k_in, vt_in, at_in, *refs):
        near_refs, far_refs, refs = refs[:sources], refs[sources : 2 * sources], refs[2 * sources :]
        out_ref, x_buf, q_buf, k_buf, vt_buf, at_buf, n_buf, *work = refs
        dom = lax.axis_index("dom")
        here = dom * (width // 2)
        there = (1 - dom) * (width // 2)
        floor = row_floor(mask_ref)
        eye = identity(tokens)
        ready = pl.ds(pl.multiple_of(here, LANES), width // 2)
        at_buf[ready, :] = at_in[ready, :]
        for l in range(layer_count):
            q_ref, k_ref, vt_ref = (q_in, k_in, vt_in) if l == 0 else (q_buf, k_buf, vt_buf)
            groups = [(there, far_refs)] if l == 0 else [(here, near_refs), (there, far_refs)]
            attend(
                groups, l, used, rows, width // heads, q_ref, k_ref, vt_ref, at_buf, work, eye, floor
            )
            together = across(eye, at_buf[...]).astype(jnp.bfloat16)
            for p in range(sources):
                n_buf[block_rows(p, rows), :] = together[p * rows : (p + 1) * rows, :]
            update = jnp.dot(n_buf[...], wo_ref[l], preferred_element_type=jnp.float32)
            before = x_ref[...] if l == 0 else x_buf[...]
            moved = (before.astype(jnp.float32) + update).astype(jnp.bfloat16)
            if l + 1 < layer_count:
                x_buf[...] = moved
                project(
                    moved, wq_ref.at[l + 1], q_buf, k_buf, vt_buf, n_buf, eye, scale, rows
                )
            else:
                for s in range(sources):
                    out_ref[s] = moved[s * rows : (s + 1) * rows, :]

    wide = pltpu.VMEM((tokens, width), jnp.bfloat16)
    tall = pltpu.VMEM((width, tokens), jnp.bfloat16)
    return pl.pallas_call(
        kernel,
        out_shape=jax.ShapeDtypeStruct((sources, rows, width), jnp.bfloat16),
        in_specs=[whole_vmem()] * (8 + 2 * sources),
        out_specs=whole_vmem(),
        scratch_shapes=[wide, wide, wide, tall, tall, wide] + work_space(heads, tokens),
        compiler_params=pltpu.CompilerParams(vmem_limit_bytes=8 * 2**20),
        cost_estimate=pl.CostEstimate(
            flops=14 * tokens * width * width, transcendentals=2 * heads * tokens * tokens,
            bytes_accessed=10 * width * width,
        ),
        name="layers",
    )(mask, w_qkv, w_out, *state, *near, *far)


def apart(joined, parts):
    pieces, at = [], 0
    for part in parts:
        pieces.append(joined[at : at + part.shape[0]])
        at += part.shape[0]
    return pieces


def spread_body(states, ancestors, noise, pair, token_mask, w_qkv, w_out, w_pair):
    particles, rows, width = states.shape
    heads = w_pair.shape[2]
    scale = (width // heads) ** (-0.5)
    swap = [(0, 1), (1, 0)]
    mask_row = token_mask.reshape(1, -1)

    def beside(block, k=1):
        return lax.ppermute(block, "tok", [(t, t ^ k) for t in range(particles)])

    other_states = lax.ppermute(states, "dom", swap)
    near, rest, own, local_noise = prepare(
        pair, mask_row, w_pair.transpose(0, 2, 1), states, noise, w_qkv
    )
    kept, neighbour, *sent = pack(ancestors, own, other_states, local_noise, near)
    ahead = rows * (width // LANES)
    passing = range(2, particles, 2)
    blocks = {k: beside(block, k) for k, block in zip(passing, sent)}
    blocks[1], blocks[3] = apart(
        beside(jnp.concatenate([neighbour, blocks[2][ahead:]], axis=0)), [neighbour, blocks[2][ahead:]]
    )
    for k in passing[1:-1]:
        blocks[k + 1] = beside(blocks[k][ahead:])
    far = {}

    def swap_all(distances):
        group = [blocks[distance] for distance in distances]
        swapped = lax.ppermute(jnp.concatenate(group, axis=0), "dom", swap)
        far.update(zip(distances, apart(swapped, group)))

    blocks[passing[-1] + 1] = beside(blocks[passing[-1]][ahead:])
    swap_all(list(passing[:-1]))
    swap_all([passing[-1]])
    swap_all(list(range(1, particles - 1, 2)))
    swap_all([particles - 1])
    swapped = [far[distance] for distance in range(1, particles)]
    blocks = [blocks[distance] for distance in range(1, particles)]
    state = first_half(mask_row, kept, near, blocks, w_qkv, rows, heads, scale)
    result = layers(
        mask_row, state, (near, *blocks), (rest, *swapped), w_qkv, w_out, rows, heads, scale
    )
    return lax.all_to_all(result, "tok", 0, 0, tiled=True)


def solution(mesh):
    placed = (
        P(("groups", "dom"), "tok", None),
        P(("groups", "dom")),
        P(("groups", "dom"), "tok", None),
        P(("groups", "tok"), None, None),
        P("groups"),
        P(),
        P(),
        P(),
    )

    def body(states, ancestors, noise, pair, token_mask, w_qkv, w_out, w_pair):
        particles, rows, width = states.shape
        fits = (
            particles == mesh.shape["tok"]
            and particles & (particles - 1) == 0
            and particles > 4
            and mesh.shape["dom"] == 2
            and width % (2 * LANES) == 0
            and w_pair.shape[2] % 2 == 0
            and pair.shape[1] == LANES
            and pair.shape[2] == LANES
            and rows % 16 == 0
            and (width // w_pair.shape[2]) % 16 == 0
        )
        chosen = spread_body if fits else gathered_body
        return chosen(states, ancestors, noise, pair, token_mask, w_qkv, w_out, w_pair)

    return jax.shard_map(
        body,
        mesh=mesh,
        in_specs=placed,
        out_specs=P(("groups", "dom"), "tok", None),
        check_vma=False,
    )
```

```python
import jax
import jax.numpy as jnp
from jax import lax
from jax.experimental import pallas as pl
from jax.experimental.pallas import tpu as pltpu
from jax.sharding import PartitionSpec as P

MASKED = -1000000000.0
LANES = 128


def layer_norm(stream):
    values = stream.astype(jnp.float32)
    average = jnp.mean(values, axis=-1, keepdims=True)
    centred = values - average
    spread = jnp.mean(centred * centred, axis=-1, keepdims=True)
    return centred * lax.rsqrt(spread + 1e-05)


def gathered_body(states, ancestors, noise, pair, token_mask, w_qkv, w_out, w_pair):
    part_count = states.shape[0]
    tok_rows = states.shape[1]
    model_width = states.shape[2]
    head_count = w_pair.shape[2]
    head_width = model_width // head_count
    layer_count = w_qkv.shape[0]
    total_keys = pair.shape[1]
    everyone = lax.all_gather(states, "dom", axis=0, tiled=True)
    chosen = jnp.take(everyone, ancestors, axis=0)
    stream = (chosen.astype(jnp.float32) + 0.5 * noise.astype(jnp.float32)).astype(jnp.bfloat16)
    penalty = jnp.where(token_mask > 0, 0.0, MASKED).astype(jnp.float32)
    pair_terms = jnp.einsum("ijc,lch->lhij", pair, w_pair, preferred_element_type=jnp.float32)
    full_bias = pair_terms + penalty[None, None, None, :]
    query_scale = head_width ** (-0.5)
    for layer_index in range(layer_count):
        normed = layer_norm(stream).astype(jnp.bfloat16)
        projected = jnp.dot(
            normed.reshape(part_count * tok_rows, model_width),
            w_qkv[layer_index],
            preferred_element_type=jnp.float32,
        )
        projected = projected.reshape(part_count, tok_rows, 3 * model_width)
        query = (projected[..., :model_width] * query_scale).astype(jnp.bfloat16)
        both = projected[..., model_width:].astype(jnp.bfloat16)
        query_heads = query.reshape(part_count, tok_rows, head_count, head_width)
        gathered = lax.all_gather(both, "tok", axis=1, tiled=True)
        all_keys, all_values = gathered[..., :model_width], gathered[..., model_width:]
        key_heads = all_keys.reshape(part_count, total_keys, head_count, head_width)
        scores = (
            jnp.einsum(
                "pihe,pjhe->phij", query_heads, key_heads, preferred_element_type=jnp.float32
            )
            + full_bias[layer_index][None]
        )
        weights = jax.nn.softmax(scores, axis=-1).astype(jnp.bfloat16)
        value_heads = all_values.reshape(part_count, total_keys, head_count, head_width)
        attended = jnp.einsum(
            "phij,pjhe->pihe", weights, value_heads, preferred_element_type=jnp.float32
        ).astype(jnp.bfloat16)
        attended = attended.reshape(part_count * tok_rows, model_width)
        update = jnp.dot(attended, w_out[layer_index], preferred_element_type=jnp.float32)
        update = update.reshape(part_count, tok_rows, model_width)
        stream = (stream.astype(jnp.float32) + update).astype(jnp.bfloat16)
    return stream


def whole_vmem():
    return pl.BlockSpec(memory_space=pltpu.VMEM)


def in_hbm():
    return pl.BlockSpec(memory_space=pltpu.HBM)


def stay(array):
    return pltpu.with_memory_space_constraint(array, pltpu.HBM)


def in_smem():
    return pl.BlockSpec(memory_space=pltpu.SMEM)


def make_bias(pair, mask_row, w_rows, w_qkv, side):
    rows, keys, channels = pair.shape
    layer_count, heads, _ = w_rows.shape
    half = heads // 2
    blocks = layer_count * half

    def kernel(pair_hbm, mask_hbm, w_hbm, wq_hbm, out_ref, pair_ref, mask_ref, w_ref, rows_ref, sem):
        copies = [
            pltpu.make_async_copy(mask_hbm, mask_ref, sem.at[0]),
            pltpu.make_async_copy(w_hbm, w_ref, sem.at[1]),
            pltpu.make_async_copy(pair_hbm, pair_ref, sem.at[2]),
        ]
        for copy in copies:
            copy.start()
        for copy in copies:
            copy.wait()
        penalty = jnp.where(mask_ref[...] > 0, 0.0, MASKED).astype(jnp.float32)
        low = lax.axis_index("dom") == side
        part = jnp.concatenate(
            [
                jnp.where(low, w[:half], w[half:])
                for w in (w_ref[l].astype(jnp.float32) for l in range(layer_count))
            ],
            axis=0,
        ).astype(jnp.bfloat16)
        terms = across(part, pair_ref[...].reshape(rows * keys, channels))
        for i in range(rows):
            piece = terms[:, i * keys : (i + 1) * keys] + penalty
            rows_ref[:, i, :] = piece - jnp.max(piece, axis=-1, keepdims=True)
        for h in range(blocks):
            out_ref[h * rows : (h + 1) * rows, :] = rows_ref[h].astype(jnp.bfloat16)

    return pl.pallas_call(
        kernel,
        out_shape=jax.ShapeDtypeStruct((blocks * rows, keys), jnp.bfloat16),
        in_specs=[in_hbm()] * 4,
        out_specs=whole_vmem(),
        scratch_shapes=[
            pltpu.VMEM(pair.shape, pair.dtype),
            pltpu.VMEM(mask_row.shape, mask_row.dtype),
            pltpu.VMEM(w_rows.shape, w_rows.dtype),
            pltpu.VMEM((blocks, rows, keys), jnp.float32),
            pltpu.SemaphoreType.DMA((3,)),
        ],
        cost_estimate=pl.CostEstimate(
            flops=2 * blocks * rows * keys * channels, transcendentals=0, bytes_accessed=8000000
        ),
        compiler_params=pltpu.CompilerParams(vmem_limit_bytes=6 * 2**20),
        name="make_bias",
    )(*(stay(a) for a in (pair, mask_row, w_rows, w_qkv)))


def block_source(position):
    return jnp.bitwise_xor(lax.axis_index("tok"), position)


def pack(ancestors, own, other, noise, bias):
    particles, rows, width = own.shape
    used = rows * (width // LANES)
    total = bias.shape[0]
    served = [0, 1] + list(range(2, particles, 2))

    def kernel(anc_ref, own_ref, other_ref, noise_ref, bias_ref, *outs):
        dom = lax.axis_index("dom")

        def put(out_ref, first, particle):
            ancestor = anc_ref[particle]
            local = lax.rem(ancestor, particles)
            mine = lax.div(ancestor, particles) == dom
            value = jnp.where(mine, own_ref[local], other_ref[local])
            value = value.astype(jnp.float32) + 0.5 * noise_ref[particle].astype(jnp.float32)
            value = value.astype(jnp.bfloat16)
            for k in range(width // LANES):
                out_ref[first + k * rows : first + (k + 1) * rows, :] = value[
                    :, k * LANES : (k + 1) * LANES
                ]

        for position, out_ref in zip(served, outs):
            put(out_ref, 0, block_source(position))
            if position > 0:
                out_ref[used : used + total, :] = bias_ref[...]
            if position > 1:
                put(out_ref, used + total, block_source(position + 1))

    lengths = [used, used + total] + [total + 2 * used] * (len(served) - 2)
    return pl.pallas_call(
        kernel,
        out_shape=tuple(jax.ShapeDtypeStruct((length, LANES), own.dtype) for length in lengths),
        in_specs=[in_smem()] + [whole_vmem()] * 4,
        out_specs=(whole_vmem(),) * len(served),
        compiler_params=pltpu.CompilerParams(vmem_limit_bytes=6 * 2**20),
        name="pack",
    )(ancestors, own, other, noise, bias)


def across(left, right):
    return lax.dot_general(
        left, right, (((1,), (1,)), ((), ())), preferred_element_type=jnp.float32
    )


def identity(size):
    down = lax.broadcasted_iota(jnp.int32, (size, size), 0)
    along = lax.broadcasted_iota(jnp.int32, (size, size), 1)
    return jnp.where(down == along, 1.0, 0.0).astype(jnp.bfloat16)


def block_rows(position, rows):
    return pl.ds(pl.multiple_of(block_source(position) * rows, rows), rows)


def project(stream, w_ref, q_ref, k_ref, vt_ref, n_ref, eye, scale, rows):
    tokens, width = stream.shape
    normed = layer_norm(stream).astype(jnp.bfloat16)
    n_ref[...] = (
        jnp.dot(normed, w_ref[:, :width], preferred_element_type=jnp.float32) * scale
    ).astype(jnp.bfloat16)
    k_ref[...] = jnp.dot(
        normed, w_ref[:, width : 2 * width], preferred_element_type=jnp.float32
    ).astype(jnp.bfloat16)
    values = jnp.dot(
        normed, w_ref[:, 2 * width :], preferred_element_type=jnp.float32
    ).astype(jnp.bfloat16)
    for t in range(0, width, LANES):
        vt_ref[t : t + LANES, :] = across(eye, values[:, t : t + LANES]).astype(jnp.bfloat16)
    for p in range(tokens // rows):
        q_ref[p * rows : (p + 1) * rows, :] = n_ref[block_rows(p, rows), :]


def attend(groups, layer, ahead, rows, head_width, q_ref, k_ref, vt_ref, at_ref, work, eye, floor):
    s_buf, e_buf, n_buf = work
    half = q_ref.shape[1] // head_width // 2
    every = [(g * half + h, h, *group) for g, group in enumerate(groups) for h in range(half)]
    for slot, h, base, blocks in every:
        low = h * head_width
        high = low + head_width
        start = low // LANES * LANES
        stop = -(-high // LANES) * LANES
        lane = lax.broadcasted_iota(jnp.int32, (1, stop - start), 1) + start
        inside = jnp.where((lane >= low) & (lane < high), 1.0, 0.0).astype(jnp.bfloat16)
        cols = pl.ds(pl.multiple_of(base + start, LANES), stop - start)
        firsts = [(layer * half + h) * rows + (0 if p == 0 or p % 2 == 1 and p > 1 else ahead) for p in range(len(blocks))]
        bias = jnp.concatenate(
            [block[at : at + rows, :] for at, block in zip(firsts, blocks)], axis=0
        )
        s_buf[slot] = across(
            jnp.concatenate([k_ref[:, cols], eye], axis=1),
            jnp.concatenate([q_ref[:, cols] * inside, bias], axis=1),
        )
    for slot, h, base, blocks in every:
        scores = s_buf[slot] + floor
        raised = jnp.exp(scores - jnp.max(scores, axis=0, keepdims=True))
        n_buf[slot : slot + 1, :] = 1.0 / jnp.sum(raised, axis=0, keepdims=True)
        e_buf[slot] = raised.astype(jnp.bfloat16)
    for slot, h, base, blocks in every:
        own = pl.ds(pl.multiple_of(base + h * head_width, 16), head_width)
        out = jnp.dot(vt_ref[own, :], e_buf[slot], preferred_element_type=jnp.float32)
        at_ref[own, :] = (out * n_buf[slot : slot + 1, :]).astype(jnp.bfloat16)


def row_floor(mask_ref):
    anyone = jnp.max(mask_ref[...], axis=-1, keepdims=True)
    return jnp.where(anyone > 0, 0.0, MASKED).astype(jnp.float32)


def work_space(slots, tokens):
    return [
        pltpu.VMEM((slots, tokens, tokens), jnp.float32),
        pltpu.VMEM((slots, tokens, tokens), jnp.bfloat16),
        pltpu.VMEM((slots, tokens), jnp.float32),
    ]


def first_half(mask, kept, near, blocks, w_qkv, rows, heads, scale):
    sources = 1 + len(blocks)
    width = w_qkv.shape[1]
    tokens = sources * rows
    used = rows * (width // LANES)
    total = near.shape[0]

    def kernel(mask_ref, w_ref, kept_ref, near_ref, *refs):
        block_refs, refs = refs[: len(blocks)], refs[len(blocks) :]
        x_ref, q_ref, k_ref, vt_ref, at_ref, n_ref, *work = refs
        for p, block in enumerate((kept_ref, *block_refs)):
            at = total if p % 2 == 1 and p > 1 else 0
            for k in range(width // LANES):
                x_ref[block_rows(p, rows), k * LANES : (k + 1) * LANES] = block[
                    at + k * rows : at + (k + 1) * rows, :
                ]
        eye = identity(tokens)
        project(x_ref[...], w_ref.at[0], q_ref, k_ref, vt_ref, n_ref, eye, scale, rows)
        here = lax.axis_index("dom") * (width // 2)
        attend(
            [(here, (near_ref, *block_refs))], 0, used, rows, width // heads,
            q_ref, k_ref, vt_ref, at_ref, work, eye, row_floor(mask_ref),
        )

    wide = jax.ShapeDtypeStruct((tokens, width), jnp.bfloat16)
    tall = jax.ShapeDtypeStruct((width, tokens), jnp.bfloat16)
    return pl.pallas_call(
        kernel,
        out_shape=(wide, wide, wide, tall, tall),
        in_specs=[whole_vmem()] * (4 + len(blocks)),
        out_specs=(whole_vmem(),) * 5,
        scratch_shapes=[pltpu.VMEM((tokens, width), jnp.bfloat16)] + work_space(heads // 2, tokens),
        compiler_params=pltpu.CompilerParams(vmem_limit_bytes=8 * 2**20),
        cost_estimate=pl.CostEstimate(
            flops=6 * tokens * width * width, transcendentals=heads * tokens * tokens // 2,
            bytes_accessed=8 * width * width,
        ),
        name="first_half",
    )(mask, w_qkv, kept, near, *blocks)


def layers(mask, state, near, far, w_qkv, w_out, rows, heads, scale):
    sources = len(near)
    layer_count, width, _ = w_qkv.shape
    tokens = sources * rows
    used = rows * (width // LANES)

    def kernel(mask_ref, wq_ref, wo_ref, x_ref, q_in, k_in, vt_in, at_in, *refs):
        near_refs, far_refs, refs = refs[:sources], refs[sources : 2 * sources], refs[2 * sources :]
        out_ref, x_buf, q_buf, k_buf, vt_buf, at_buf, n_buf, *work = refs
        dom = lax.axis_index("dom")
        here = dom * (width // 2)
        there = (1 - dom) * (width // 2)
        floor = row_floor(mask_ref)
        eye = identity(tokens)
        ready = pl.ds(pl.multiple_of(here, LANES), width // 2)
        at_buf[ready, :] = at_in[ready, :]
        for l in range(layer_count):
            q_ref, k_ref, vt_ref = (q_in, k_in, vt_in) if l == 0 else (q_buf, k_buf, vt_buf)
            groups = [(there, far_refs)] if l == 0 else [(here, near_refs), (there, far_refs)]
            attend(
                groups, l, used, rows, width // heads, q_ref, k_ref, vt_ref, at_buf, work, eye, floor
            )
            together = across(eye, at_buf[...]).astype(jnp.bfloat16)
            for p in range(sources):
                n_buf[block_rows(p, rows), :] = together[p * rows : (p + 1) * rows, :]
            update = jnp.dot(n_buf[...], wo_ref[l], preferred_element_type=jnp.float32)
            before = x_ref[...] if l == 0 else x_buf[...]
            moved = (before.astype(jnp.float32) + update).astype(jnp.bfloat16)
            if l + 1 < layer_count:
                x_buf[...] = moved
                project(
                    moved, wq_ref.at[l + 1], q_buf, k_buf, vt_buf, n_buf, eye, scale, rows
                )
            else:
                for s in range(sources):
                    out_ref[s] = moved[s * rows : (s + 1) * rows, :]

    wide = pltpu.VMEM((tokens, width), jnp.bfloat16)
    tall = pltpu.VMEM((width, tokens), jnp.bfloat16)
    return pl.pallas_call(
        kernel,
        out_shape=jax.ShapeDtypeStruct((sources, rows, width), jnp.bfloat16),
        in_specs=[whole_vmem()] * (8 + 2 * sources),
        out_specs=whole_vmem(),
        scratch_shapes=[wide, wide, wide, tall, tall, wide] + work_space(heads, tokens),
        compiler_params=pltpu.CompilerParams(vmem_limit_bytes=8 * 2**20),
        cost_estimate=pl.CostEstimate(
            flops=14 * tokens * width * width, transcendentals=2 * heads * tokens * tokens,
            bytes_accessed=10 * width * width,
        ),
        name="layers",
    )(mask, w_qkv, w_out, *state, *near, *far)


def apart(joined, parts):
    pieces, at = [], 0
    for part in parts:
        pieces.append(joined[at : at + part.shape[0]])
        at += part.shape[0]
    return pieces


def spread_body(states, ancestors, noise, pair, token_mask, w_qkv, w_out, w_pair):
    particles, rows, width = states.shape
    heads = w_pair.shape[2]
    scale = (width // heads) ** (-0.5)
    swap = [(0, 1), (1, 0)]
    mask_row = token_mask.reshape(1, -1)

    def beside(block, k=1):
        return lax.ppermute(block, "tok", [(t, t ^ k) for t in range(particles)])

    other_states = lax.ppermute(states, "dom", swap)
    w_rows = w_pair.transpose(0, 2, 1)
    near = make_bias(pair, mask_row, w_rows, w_qkv, 0)
    kept, neighbour, *sent = pack(ancestors, states, other_states, noise, near)
    ahead = rows * (width // LANES)
    passing = range(2, particles, 2)
    late_pair, _ = lax.optimization_barrier((pair, kept))
    rest = make_bias(late_pair, mask_row, w_rows, w_qkv, 1)
    blocks = {k: beside(block, k) for k, block in zip(passing, sent)}
    blocks[1], blocks[3] = apart(
        beside(jnp.concatenate([neighbour, blocks[2][ahead:]], axis=0)), [neighbour, blocks[2][ahead:]]
    )
    for k in passing[1:-1]:
        blocks[k + 1] = beside(blocks[k][ahead:])
    far = {}

    def swap_all(distances):
        group = [blocks[distance] for distance in distances]
        swapped = lax.ppermute(jnp.concatenate(group, axis=0), "dom", swap)
        far.update(zip(distances, apart(swapped, group)))

    blocks[passing[-1] + 1] = beside(blocks[passing[-1]][ahead:])
    swap_all(list(passing[:-1]))
    swap_all([passing[-1]])
    swap_all(list(range(1, particles - 1, 2)))
    swap_all([particles - 1])
    swapped = [far[distance] for distance in range(1, particles)]
    blocks = [blocks[distance] for distance in range(1, particles)]
    state = first_half(mask_row, kept, near, blocks, w_qkv, rows, heads, scale)
    result = layers(
        mask_row, state, (near, *blocks), (rest, *swapped), w_qkv, w_out, rows, heads, scale
    )
    return lax.all_to_all(result, "tok", 0, 0, tiled=True)


def solution(mesh):
    placed = (
        P(("groups", "dom"), "tok", None),
        P(("groups", "dom")),
        P(("groups", "dom"), "tok", None),
        P(("groups", "tok"), None, None),
        P("groups"),
        P(),
        P(),
        P(),
    )

    def body(states, ancestors, noise, pair, token_mask, w_qkv, w_out, w_pair):
        particles, rows, width = states.shape
        fits = (
            particles == mesh.shape["tok"]
            and particles & (particles - 1) == 0
            and particles > 4
            and mesh.shape["dom"] == 2
            and width % (2 * LANES) == 0
            and w_pair.shape[2] % 2 == 0
            and pair.shape[1] == LANES
            and pair.shape[2] == LANES
            and rows % 16 == 0
            and (width // w_pair.shape[2]) % 16 == 0
        )
        chosen = spread_body if fits else gathered_body
        return chosen(states, ancestors, noise, pair, token_mask, w_qkv, w_out, w_pair)

    return jax.shard_map(
        body,
        mesh=mesh,
        in_specs=placed,
        out_specs=P(("groups", "dom"), "tok", None),
        check_vma=False,
    )
```

```python
import jax
import jax.numpy as jnp
from jax import lax
from jax.experimental import pallas as pl
from jax.experimental.pallas import tpu as pltpu
from jax.sharding import PartitionSpec as P

MASKED = -1000000000.0
LANES = 128


def layer_norm(stream):
    values = stream.astype(jnp.float32)
    average = jnp.mean(values, axis=-1, keepdims=True)
    centred = values - average
    spread = jnp.mean(centred * centred, axis=-1, keepdims=True)
    return centred * lax.rsqrt(spread + 1e-05)


def gathered_body(states, ancestors, noise, pair, token_mask, w_qkv, w_out, w_pair):
    part_count = states.shape[0]
    tok_rows = states.shape[1]
    model_width = states.shape[2]
    head_count = w_pair.shape[2]
    head_width = model_width // head_count
    layer_count = w_qkv.shape[0]
    total_keys = pair.shape[1]
    everyone = lax.all_gather(states, "dom", axis=0, tiled=True)
    chosen = jnp.take(everyone, ancestors, axis=0)
    stream = (chosen.astype(jnp.float32) + 0.5 * noise.astype(jnp.float32)).astype(jnp.bfloat16)
    penalty = jnp.where(token_mask > 0, 0.0, MASKED).astype(jnp.float32)
    pair_terms = jnp.einsum("ijc,lch->lhij", pair, w_pair, preferred_element_type=jnp.float32)
    full_bias = pair_terms + penalty[None, None, None, :]
    query_scale = head_width ** (-0.5)
    for layer_index in range(layer_count):
        normed = layer_norm(stream).astype(jnp.bfloat16)
        projected = jnp.dot(
            normed.reshape(part_count * tok_rows, model_width),
            w_qkv[layer_index],
            preferred_element_type=jnp.float32,
        )
        projected = projected.reshape(part_count, tok_rows, 3 * model_width)
        query = (projected[..., :model_width] * query_scale).astype(jnp.bfloat16)
        both = projected[..., model_width:].astype(jnp.bfloat16)
        query_heads = query.reshape(part_count, tok_rows, head_count, head_width)
        gathered = lax.all_gather(both, "tok", axis=1, tiled=True)
        all_keys, all_values = gathered[..., :model_width], gathered[..., model_width:]
        key_heads = all_keys.reshape(part_count, total_keys, head_count, head_width)
        scores = (
            jnp.einsum(
                "pihe,pjhe->phij", query_heads, key_heads, preferred_element_type=jnp.float32
            )
            + full_bias[layer_index][None]
        )
        weights = jax.nn.softmax(scores, axis=-1).astype(jnp.bfloat16)
        value_heads = all_values.reshape(part_count, total_keys, head_count, head_width)
        attended = jnp.einsum(
            "phij,pjhe->pihe", weights, value_heads, preferred_element_type=jnp.float32
        ).astype(jnp.bfloat16)
        attended = attended.reshape(part_count * tok_rows, model_width)
        update = jnp.dot(attended, w_out[layer_index], preferred_element_type=jnp.float32)
        update = update.reshape(part_count, tok_rows, model_width)
        stream = (stream.astype(jnp.float32) + update).astype(jnp.bfloat16)
    return stream


def whole_vmem():
    return pl.BlockSpec(memory_space=pltpu.VMEM)


def in_hbm():
    return pl.BlockSpec(memory_space=pltpu.HBM)


def stay(array):
    return pltpu.with_memory_space_constraint(array, pltpu.HBM)


def in_smem():
    return pl.BlockSpec(memory_space=pltpu.SMEM)


def make_bias(pair, mask_row, w_rows, w_qkv, side):
    rows, keys, channels = pair.shape
    layer_count, heads, _ = w_rows.shape
    half = heads // 2
    blocks = layer_count * half

    def kernel(pair_hbm, mask_hbm, w_hbm, wq_hbm, out_ref, pair_ref, mask_ref, w_ref, rows_ref, sem):
        copies = [
            pltpu.make_async_copy(mask_hbm, mask_ref, sem.at[0]),
            pltpu.make_async_copy(w_hbm, w_ref, sem.at[1]),
            pltpu.make_async_copy(pair_hbm, pair_ref, sem.at[2]),
        ]
        for copy in copies:
            copy.start()
        for copy in copies:
            copy.wait()
        penalty = jnp.where(mask_ref[...] > 0, 0.0, MASKED).astype(jnp.float32)
        low = lax.axis_index("dom") == side
        part = jnp.concatenate(
            [
                jnp.where(low, w[:half], w[half:])
                for w in (w_ref[l].astype(jnp.float32) for l in range(layer_count))
            ],
            axis=0,
        ).astype(jnp.bfloat16)
        terms = across(part, pair_ref[...].reshape(rows * keys, channels))
        for i in range(rows):
            piece = terms[:, i * keys : (i + 1) * keys] + penalty
            rows_ref[:, i, :] = piece - jnp.max(piece, axis=-1, keepdims=True)
        for h in range(blocks):
            out_ref[h * rows : (h + 1) * rows, :] = rows_ref[h].astype(jnp.bfloat16)

    return pl.pallas_call(
        kernel,
        out_shape=jax.ShapeDtypeStruct((blocks * rows, keys), jnp.bfloat16),
        in_specs=[in_hbm()] * 4,
        out_specs=whole_vmem(),
        scratch_shapes=[
            pltpu.VMEM(pair.shape, pair.dtype),
            pltpu.VMEM(mask_row.shape, mask_row.dtype),
            pltpu.VMEM(w_rows.shape, w_rows.dtype),
            pltpu.VMEM((blocks, rows, keys), jnp.float32),
            pltpu.SemaphoreType.DMA((3,)),
        ],
        cost_estimate=pl.CostEstimate(
            flops=2 * blocks * rows * keys * channels, transcendentals=0, bytes_accessed=8000000
        ),
        compiler_params=pltpu.CompilerParams(vmem_limit_bytes=6 * 2**20),
        name="make_bias",
    )(*(stay(a) for a in (pair, mask_row, w_rows, w_qkv)))


def block_source(position):
    return jnp.bitwise_xor(lax.axis_index("tok"), position)


def pack(ancestors, own, other, noise, bias):
    particles, rows, width = own.shape
    used = rows * (width // LANES)
    total = bias.shape[0]
    served = [0, 1] + list(range(2, particles, 2))

    def kernel(anc_ref, own_ref, other_ref, noise_ref, bias_ref, *outs):
        dom = lax.axis_index("dom")

        def put(out_ref, first, particle):
            ancestor = anc_ref[particle]
            local = lax.rem(ancestor, particles)
            mine = lax.div(ancestor, particles) == dom
            value = jnp.where(mine, own_ref[local], other_ref[local])
            value = value.astype(jnp.float32) + 0.5 * noise_ref[particle].astype(jnp.float32)
            value = value.astype(jnp.bfloat16)
            for k in range(width // LANES):
                out_ref[first + k * rows : first + (k + 1) * rows, :] = value[
                    :, k * LANES : (k + 1) * LANES
                ]

        for position, out_ref in zip(served, outs):
            put(out_ref, 0, block_source(position))
            if position > 0:
                out_ref[used : used + total, :] = bias_ref[...]
            if position > 1:
                put(out_ref, used + total, block_source(position + 1))

    lengths = [used, used + total] + [total + 2 * used] * (len(served) - 2)
    return pl.pallas_call(
        kernel,
        out_shape=tuple(jax.ShapeDtypeStruct((length, LANES), own.dtype) for length in lengths),
        in_specs=[in_smem()] + [whole_vmem()] * 4,
        out_specs=(whole_vmem(),) * len(served),
        compiler_params=pltpu.CompilerParams(vmem_limit_bytes=6 * 2**20),
        name="pack",
    )(ancestors, own, other, noise, bias)


def across(left, right):
    return lax.dot_general(
        left, right, (((1,), (1,)), ((), ())), preferred_element_type=jnp.float32
    )


def identity(size):
    down = lax.broadcasted_iota(jnp.int32, (size, size), 0)
    along = lax.broadcasted_iota(jnp.int32, (size, size), 1)
    return jnp.where(down == along, 1.0, 0.0).astype(jnp.bfloat16)


def block_rows(position, rows):
    return pl.ds(pl.multiple_of(block_source(position) * rows, rows), rows)


def project(stream, w_ref, q_ref, k_ref, vt_ref, n_ref, eye, scale, rows):
    tokens, width = stream.shape
    normed = layer_norm(stream).astype(jnp.bfloat16)
    n_ref[...] = (
        jnp.dot(normed, w_ref[:, :width], preferred_element_type=jnp.float32) * scale
    ).astype(jnp.bfloat16)
    k_ref[...] = jnp.dot(
        normed, w_ref[:, width : 2 * width], preferred_element_type=jnp.float32
    ).astype(jnp.bfloat16)
    values = jnp.dot(
        normed, w_ref[:, 2 * width :], preferred_element_type=jnp.float32
    ).astype(jnp.bfloat16)
    for t in range(0, width, LANES):
        vt_ref[t : t + LANES, :] = across(eye, values[:, t : t + LANES]).astype(jnp.bfloat16)
    for p in range(tokens // rows):
        q_ref[p * rows : (p + 1) * rows, :] = n_ref[block_rows(p, rows), :]


def attend(groups, layer, ahead, rows, head_width, q_ref, k_ref, vt_ref, at_ref, work, eye, floor):
    s_buf, e_buf, n_buf = work
    half = q_ref.shape[1] // head_width // 2
    every = [(g * half + h, h, *group) for g, group in enumerate(groups) for h in range(half)]
    for slot, h, base, blocks in every:
        low = h * head_width
        high = low + head_width
        start = low // LANES * LANES
        stop = -(-high // LANES) * LANES
        lane = lax.broadcasted_iota(jnp.int32, (1, stop - start), 1) + start
        inside = jnp.where((lane >= low) & (lane < high), 1.0, 0.0).astype(jnp.bfloat16)
        cols = pl.ds(pl.multiple_of(base + start, LANES), stop - start)
        firsts = [(layer * half + h) * rows + (0 if p == 0 or p % 2 == 1 and p > 1 else ahead) for p in range(len(blocks))]
        bias = jnp.concatenate(
            [block[at : at + rows, :] for at, block in zip(firsts, blocks)], axis=0
        )
        s_buf[slot] = across(
            jnp.concatenate([k_ref[:, cols], eye], axis=1),
            jnp.concatenate([q_ref[:, cols] * inside, bias], axis=1),
        )
    for slot, h, base, blocks in every:
        scores = s_buf[slot] + floor
        raised = jnp.exp(scores - jnp.max(scores, axis=0, keepdims=True))
        n_buf[slot : slot + 1, :] = 1.0 / jnp.sum(raised, axis=0, keepdims=True)
        e_buf[slot] = raised.astype(jnp.bfloat16)
    for slot, h, base, blocks in every:
        own = pl.ds(pl.multiple_of(base + h * head_width, 16), head_width)
        out = jnp.dot(vt_ref[own, :], e_buf[slot], preferred_element_type=jnp.float32)
        at_ref[own, :] = (out * n_buf[slot : slot + 1, :]).astype(jnp.bfloat16)


def row_floor(mask_ref):
    anyone = jnp.max(mask_ref[...], axis=-1, keepdims=True)
    return jnp.where(anyone > 0, 0.0, MASKED).astype(jnp.float32)


def work_space(slots, tokens):
    return [
        pltpu.VMEM((slots, tokens, tokens), jnp.float32),
        pltpu.VMEM((slots, tokens, tokens), jnp.bfloat16),
        pltpu.VMEM((slots, tokens), jnp.float32),
    ]


def first_half(mask, kept, near, blocks, w_qkv, rows, heads, scale):
    sources = 1 + len(blocks)
    width = w_qkv.shape[1]
    tokens = sources * rows
    used = rows * (width // LANES)
    total = near.shape[0]

    def kernel(mask_ref, w_ref, kept_ref, near_ref, *refs):
        block_refs, refs = refs[: len(blocks)], refs[len(blocks) :]
        x_ref, q_ref, k_ref, vt_ref, at_ref, n_ref, *work = refs
        for p, block in enumerate((kept_ref, *block_refs)):
            at = total if p % 2 == 1 and p > 1 else 0
            for k in range(width // LANES):
                x_ref[block_rows(p, rows), k * LANES : (k + 1) * LANES] = block[
                    at + k * rows : at + (k + 1) * rows, :
                ]
        eye = identity(tokens)
        project(x_ref[...], w_ref.at[0], q_ref, k_ref, vt_ref, n_ref, eye, scale, rows)
        here = lax.axis_index("dom") * (width // 2)
        attend(
            [(here, (near_ref, *block_refs))], 0, used, rows, width // heads,
            q_ref, k_ref, vt_ref, at_ref, work, eye, row_floor(mask_ref),
        )

    wide = jax.ShapeDtypeStruct((tokens, width), jnp.bfloat16)
    tall = jax.ShapeDtypeStruct((width, tokens), jnp.bfloat16)
    return pl.pallas_call(
        kernel,
        out_shape=(wide, wide, wide, tall, tall),
        in_specs=[whole_vmem()] * (4 + len(blocks)),
        out_specs=(whole_vmem(),) * 5,
        scratch_shapes=[pltpu.VMEM((tokens, width), jnp.bfloat16)] + work_space(heads // 2, tokens),
        compiler_params=pltpu.CompilerParams(vmem_limit_bytes=8 * 2**20),
        cost_estimate=pl.CostEstimate(
            flops=6 * tokens * width * width, transcendentals=heads * tokens * tokens // 2,
            bytes_accessed=8 * width * width,
        ),
        name="first_half",
    )(mask, w_qkv, kept, near, *blocks)


def layers(mask, state, near, far, w_qkv, w_out, rows, heads, scale):
    sources = len(near)
    layer_count, width, _ = w_qkv.shape
    tokens = sources * rows
    used = rows * (width // LANES)

    def kernel(mask_ref, wq_ref, wo_ref, x_ref, q_in, k_in, vt_in, at_in, *refs):
        near_refs, far_refs, refs = refs[:sources], refs[sources : 2 * sources], refs[2 * sources :]
        out_ref, x_buf, q_buf, k_buf, vt_buf, at_buf, n_buf, *work = refs
        dom = lax.axis_index("dom")
        here = dom * (width // 2)
        there = (1 - dom) * (width // 2)
        floor = row_floor(mask_ref)
        eye = identity(tokens)
        ready = pl.ds(pl.multiple_of(here, LANES), width // 2)
        at_buf[ready, :] = at_in[ready, :]
        for l in range(layer_count):
            q_ref, k_ref, vt_ref = (q_in, k_in, vt_in) if l == 0 else (q_buf, k_buf, vt_buf)
            groups = [(there, far_refs)] if l == 0 else [(here, near_refs), (there, far_refs)]
            attend(
                groups, l, used, rows, width // heads, q_ref, k_ref, vt_ref, at_buf, work, eye, floor
            )
            together = across(eye, at_buf[...]).astype(jnp.bfloat16)
            for p in range(sources):
                n_buf[block_rows(p, rows), :] = together[p * rows : (p + 1) * rows, :]
            update = jnp.dot(n_buf[...], wo_ref[l], preferred_element_type=jnp.float32)
            before = x_ref[...] if l == 0 else x_buf[...]
            moved = (before.astype(jnp.float32) + update).astype(jnp.bfloat16)
            if l + 1 < layer_count:
                x_buf[...] = moved
                project(
                    moved, wq_ref.at[l + 1], q_buf, k_buf, vt_buf, n_buf, eye, scale, rows
                )
            else:
                for s in range(sources):
                    out_ref[s] = moved[s * rows : (s + 1) * rows, :]

    wide = pltpu.VMEM((tokens, width), jnp.bfloat16)
    tall = pltpu.VMEM((width, tokens), jnp.bfloat16)
    return pl.pallas_call(
        kernel,
        out_shape=jax.ShapeDtypeStruct((sources, rows, width), jnp.bfloat16),
        in_specs=[whole_vmem()] * (8 + 2 * sources),
        out_specs=whole_vmem(),
        scratch_shapes=[wide, wide, wide, tall, tall, wide] + work_space(heads, tokens),
        compiler_params=pltpu.CompilerParams(vmem_limit_bytes=8 * 2**20),
        cost_estimate=pl.CostEstimate(
            flops=14 * tokens * width * width, transcendentals=2 * heads * tokens * tokens,
            bytes_accessed=10 * width * width,
        ),
        name="layers",
    )(mask, w_qkv, w_out, *state, *near, *far)


def apart(joined, parts):
    pieces, at = [], 0
    for part in parts:
        pieces.append(joined[at : at + part.shape[0]])
        at += part.shape[0]
    return pieces


def spread_body(states, ancestors, noise, pair, token_mask, w_qkv, w_out, w_pair):
    particles, rows, width = states.shape
    heads = w_pair.shape[2]
    scale = (width // heads) ** (-0.5)
    swap = [(0, 1), (1, 0)]
    mask_row = token_mask.reshape(1, -1)

    def beside(block, k=1):
        return lax.ppermute(block, "tok", [(t, t ^ k) for t in range(particles)])

    other_states = lax.ppermute(states, "dom", swap)
    w_rows = w_pair.transpose(0, 2, 1)
    near = make_bias(pair, mask_row, w_rows, w_qkv, 0)
    kept, neighbour, *sent = pack(ancestors, states, other_states, noise, near)
    ahead = rows * (width // LANES)
    passing = range(2, particles, 2)
    late_pair, _ = lax.optimization_barrier((pair, kept))
    rest = make_bias(late_pair, mask_row, w_rows, w_qkv, 1)
    blocks = {k: beside(block, k) for k, block in zip(passing, sent)}
    blocks[1], blocks[3] = apart(
        beside(jnp.concatenate([neighbour, blocks[2][ahead:]], axis=0)), [neighbour, blocks[2][ahead:]]
    )
    for k in passing[1:-1]:
        blocks[k + 1] = beside(blocks[k][ahead:])
    far = {}

    def swap_all(distances):
        group = [blocks[distance] for distance in distances]
        swapped = lax.ppermute(jnp.concatenate(group, axis=0), "dom", swap)
        far.update(zip(distances, apart(swapped, group)))

    blocks[passing[-1] + 1] = beside(blocks[passing[-1]][ahead:])
    swap_all(list(passing[:-1]))
    swap_all([passing[-1]] + list(range(1, particles - 3, 2)))
    swap_all([particles - 3])
    swap_all([particles - 1])
    swapped = [far[distance] for distance in range(1, particles)]
    blocks = [blocks[distance] for distance in range(1, particles)]
    state = first_half(mask_row, kept, near, blocks, w_qkv, rows, heads, scale)
    result = layers(
        mask_row, state, (near, *blocks), (rest, *swapped), w_qkv, w_out, rows, heads, scale
    )
    return lax.all_to_all(result, "tok", 0, 0, tiled=True)


def solution(mesh):
    placed = (
        P(("groups", "dom"), "tok", None),
        P(("groups", "dom")),
        P(("groups", "dom"), "tok", None),
        P(("groups", "tok"), None, None),
        P("groups"),
        P(),
        P(),
        P(),
    )

    def body(states, ancestors, noise, pair, token_mask, w_qkv, w_out, w_pair):
        particles, rows, width = states.shape
        fits = (
            particles == mesh.shape["tok"]
            and particles & (particles - 1) == 0
            and particles > 4
            and mesh.shape["dom"] == 2
            and width % (2 * LANES) == 0
            and w_pair.shape[2] % 2 == 0
            and pair.shape[1] == LANES
            and pair.shape[2] == LANES
            and rows % 16 == 0
            and (width // w_pair.shape[2]) % 16 == 0
        )
        chosen = spread_body if fits else gathered_body
        return chosen(states, ancestors, noise, pair, token_mask, w_qkv, w_out, w_pair)

    return jax.shard_map(
        body,
        mesh=mesh,
        in_specs=placed,
        out_specs=P(("groups", "dom"), "tok", None),
        check_vma=False,
    )
```
